32 devices in a mesh: groups: 2 (over x), freq: 16 (over z, y, core).
Axes of the slice: x: 2, y: 2, z: 4, core: 2. Of those that a mesh axis runs over, the one named last changes fastest.
Arguments:
- dyson: bfloat16 [128, 4, 2, 512, 512], P(('groups', 'freq')), parts along dimension 0, may hold values from -2.1 to 2.1
- guess: bfloat16 [128, 4, 2, 512, 512], P(('groups', 'freq')), parts along dimension 0, may hold values from -2 to 2
- coulomb: bfloat16 [1024, 512], P('groups'), parts along dimension 0, may hold values from -3 to 3
- partner: int32 [4], replicated, may hold values from 0 to 3, as said below
- freq_index: int32 [2, 64], replicated, may hold values from -128 to 127
Outputs:
- screened: bfloat16 [128, 4, 2, 512, 512], P(('groups', 'freq')), parts along dimension 0
The draws below stay inside these ranges and needn't reach their ends.
There are 2 independent parts, one for each index of `groups`. The reference program is written for one: setup_inputs(seed, part) draws one part's arguments, and reference() takes and returns one part's arrays. A program takes and returns all parts, laid end to end along the dimension named above; an argument that names none is the same for every part. Nothing has to cross between parts.
Inputs may be any that keep to these rules, and one draw needn't show every extreme that they name: partner is a permutation of the 4 lattice vectors.
All inputs are finite; a program needn't handle non-finite values.
Results may differ from the reference program's by a relative error of at most 0.0069.
Values may be sent and summed in bfloat16 or wider, within the bound.
A program may use at most 256 MiB of HBM per device.

```python
import math
import jax
import jax.numpy as jnp
from jax import lax

M = 512
NW = 64
NT = 64
NR = 4


def common_fields(key):
    bit_count = M.bit_length() - 1
    angles = jax.random.uniform(jax.random.fold_in(key, 31), (NR, bit_count), minval=0.3, maxval=1.27)
    indices = jnp.arange(M)
    ortho = jnp.ones((NR, M, M), jnp.float32)
    for level in range(bit_count):
        bit_value = indices // 2 ** level % 2
        same_bit = (bit_value[:, None] == bit_value[None, :])[None]
        lower_bit = (bit_value[:, None] < bit_value[None, :])[None]
        cosine = jnp.cos(angles[:, level])[:, None, None]
        sine_part = jnp.sin(angles[:, level])[:, None, None]
        ortho = ortho * jnp.where(same_bit, cosine, jnp.where(lower_bit, sine_part, -sine_part))
    magnitude = jnp.exp(jax.random.uniform(jax.random.fold_in(key, 32), (NW, NR, M), minval=math.log(0.5), maxval=math.log(2.0)))
    phases = jax.random.uniform(jax.random.fold_in(key, 33), (NW, NR, M), minval=-math.pi, maxval=math.pi)
    return (ortho, magnitude, phases)


def draw_dyson(key, part):
    ortho, magnitude, phases = common_fields(key)
    noise_scale = 0.15 / math.sqrt(M)
    noise = jnp.clip(jax.random.normal(jax.random.fold_in(key, 34), (NW, NR, 2, M, M)), -6.0, 6.0) * noise_scale
    real_part = ortho[None] * (magnitude * jnp.cos(phases))[:, :, None, :]
    imag_part = ortho[None] * (magnitude * jnp.sin(phases))[:, :, None, :]
    return (jnp.stack([real_part, imag_part], axis=2) + noise).astype(jnp.bfloat16)


def draw_guess(key, part):
    ortho, magnitude, phases = common_fields(key)
    turned = jnp.swapaxes(ortho, 1, 2)[None]
    real_part = turned * (jnp.cos(phases) / magnitude)[:, :, :, None]
    imag_part = -turned * (jnp.sin(phases) / magnitude)[:, :, :, None]
    return jnp.stack([real_part, imag_part], axis=2).astype(jnp.bfloat16)


def draw_partner(key, part):
    return jax.random.permutation(jax.random.fold_in(key, 21), NR).astype(jnp.int32)


def place_ends(values, stream_key, low, high):
    index_at = [jax.random.randint(jax.random.fold_in(stream_key, axis), (), 0, length) for axis, length in enumerate(values.shape)]
    longest = values.shape.index(max(values.shape))
    next_to = index_at[:longest] + [(index_at[longest] + 1) % values.shape[longest]] + index_at[longest + 1:]
    return values.at[tuple(index_at)].set(low).at[tuple(next_to)].set(high)


def bell_draw(rng, shape, width, bound, kind=jnp.bfloat16):
    values = width * jax.random.normal(rng, shape, jnp.float32)
    return jnp.clip(values, min=-bound, max=bound).astype(kind)


def setup_inputs(seed: int = 0, part: int = 0) -> dict:
    streams_of = jax.random.split(jax.random.key(seed), 6)
    part_splits = jax.random.split(jax.random.fold_in(streams_of[5], part), 6)
    dyson = draw_dyson(jax.random.fold_in(jax.random.fold_in(streams_of[5], part), 71), part)
    guess = draw_guess(jax.random.fold_in(jax.random.fold_in(streams_of[5], part), 71), part)
    coulomb = bell_draw(part_splits[2], (M, M), 0.5, 3.0)
    partner = draw_partner(jax.random.fold_in(streams_of[5], 71), part)
    freq_index = place_ends(jax.random.randint(streams_of[4], (2, NW), -2 * NW, 2 * NW), jax.random.fold_in(streams_of[4], 1), -2 * NW, (2 * NW) - 1).astype(jnp.int32)
    return {"dyson": dyson, "guess": guess, "coulomb": coulomb, "partner": partner, "freq_index": freq_index}


def fermion_table(freq_index, time_count):
    freq_count = freq_index.shape[1]
    odd_freq = 2 * freq_index[0] + 1
    odd_time = 2 * jnp.arange(time_count, dtype=jnp.int32) + 1
    phases = jnp.mod(odd_time[:, None] * odd_freq[None, :], 4 * time_count)
    angles = phases.astype(jnp.float32) * (math.pi / (2 * time_count))
    cosine = jnp.cos(angles) / math.sqrt(freq_count)
    sine_part = jnp.sin(angles) / math.sqrt(freq_count)
    real_rows = jnp.stack([cosine, sine_part], axis=-1)
    imag_rows = jnp.stack([-sine_part, cosine], axis=-1)
    return jnp.stack([real_rows, imag_rows], axis=1).astype(jnp.bfloat16)

def boson_table(freq_index, time_count):
    odd_time = 2 * jnp.arange(time_count, dtype=jnp.int32) + 1
    phases = jnp.mod(freq_index[1][:, None] * odd_time[None, :], 2 * time_count)
    angles = phases.astype(jnp.float32) * (math.pi / time_count)
    cosine = jnp.cos(angles) / math.sqrt(time_count)
    sine_part = jnp.sin(angles) / math.sqrt(time_count)
    real_rows = jnp.stack([cosine, -sine_part], axis=-1)
    imag_rows = jnp.stack([sine_part, cosine], axis=-1)
    return jnp.stack([real_rows, imag_rows], axis=1).astype(jnp.bfloat16)

def matrix_dot(left_matrix, right_matrix):
    return jnp.dot(left_matrix, right_matrix, preferred_element_type=jnp.float32)

def newton_matrix(dyson_one, guess_one):
    dyson_real, dyson_imag = (dyson_one[0], dyson_one[1])
    guess_real, guess_imag = (guess_one[0], guess_one[1])
    product_real = matrix_dot(dyson_real, guess_real) - matrix_dot(dyson_imag, guess_imag)
    product_imag = matrix_dot(dyson_real, guess_imag) + matrix_dot(dyson_imag, guess_real)
    unit_matrix = jnp.eye(dyson_real.shape[0], dtype=jnp.float32)
    corr_real = (2.0 * unit_matrix - product_real).astype(jnp.bfloat16)
    corr_imag = (-product_imag).astype(jnp.bfloat16)
    green_real = matrix_dot(guess_real, corr_real) - matrix_dot(guess_imag, corr_imag)
    green_imag = matrix_dot(guess_real, corr_imag) + matrix_dot(guess_imag, corr_real)
    return jnp.stack([green_real, green_imag]).astype(jnp.bfloat16)

def reference(dyson, guess, coulomb, partner, freq_index):
    forward = fermion_table(freq_index, NT).astype(jnp.float32)
    backward = boson_table(freq_index, NT).astype(jnp.float32)

    def newton_frequency(inputs):
        dyson_freq, guess_freq = inputs
        return jnp.stack([newton_matrix(dyson_freq[vector], guess_freq[vector]) for vector in range(NR)])
    green = lax.map(newton_frequency, (dyson, guess))
    hole = jnp.swapaxes(jnp.take(green, partner, axis=1), -1, -2)

    def polar_vector(inputs):
        green_vec, hole_vec = inputs
        green_time = jnp.einsum('tdwc,wcij->tdij', forward, green_vec.astype(jnp.float32), precision=lax.Precision.HIGHEST)
        hole_time = jnp.einsum('tdwc,wcij->tdij', forward, hole_vec.astype(jnp.float32), precision=lax.Precision.HIGHEST)
        hole_time = hole_time[::-1]
        polar_real = green_time[:, 0] * hole_time[:, 0] - green_time[:, 1] * hole_time[:, 1]
        polar_imag = green_time[:, 0] * hole_time[:, 1] + green_time[:, 1] * hole_time[:, 0]
        polar = jnp.stack([polar_real, polar_imag], axis=1).astype(jnp.bfloat16)
        polar_freq = jnp.einsum('vdtc,tcij->vdij', backward, polar.astype(jnp.float32), precision=lax.Precision.HIGHEST)
        return polar_freq.astype(jnp.bfloat16)
    polar_all = lax.map(polar_vector, (jnp.swapaxes(green, 0, 1), jnp.swapaxes(hole, 0, 1)))
    polar_all = jnp.swapaxes(polar_all, 0, 1)
    coulomb_wide = coulomb.astype(jnp.float32)

    def screen_frequency(polar_freq):
        results = []
        for vector in range(NR):
            vp_real = matrix_dot(coulomb, polar_freq[vector, 0]).astype(jnp.bfloat16)
            vp_imag = matrix_dot(coulomb, polar_freq[vector, 1]).astype(jnp.bfloat16)
            screen_real = coulomb_wide + matrix_dot(vp_real, coulomb)
            screen_imag = matrix_dot(vp_imag, coulomb)
            results.append(jnp.stack([screen_real, screen_imag]))
        return jnp.stack(results).astype(jnp.bfloat16)
    return lax.map(screen_frequency, polar_all)
```

```python
import functools
import math

import jax
import jax.numpy as jnp
from jax import lax
from jax.experimental import pallas as pl
from jax.experimental.pallas import tpu as pltpu
from jax.sharding import PartitionSpec as P

NT = 64


def fermion_table(freq_index, time_count):
    freq_count = freq_index.shape[1]
    odd_freq = 2 * freq_index[0] + 1
    odd_time = 2 * jnp.arange(time_count, dtype=jnp.int32) + 1
    phases = jnp.mod(odd_time[:, None] * odd_freq[None, :], 4 * time_count)
    angles = phases.astype(jnp.float32) * (math.pi / (2 * time_count))
    cosine = jnp.cos(angles) / math.sqrt(freq_count)
    sine_part = jnp.sin(angles) / math.sqrt(freq_count)
    real_rows = jnp.stack([cosine, sine_part], axis=-1)
    imag_rows = jnp.stack([-sine_part, cosine], axis=-1)
    return jnp.stack([real_rows, imag_rows], axis=1).astype(jnp.bfloat16)


def boson_table(freq_index, time_count):
    odd_time = 2 * jnp.arange(time_count, dtype=jnp.int32) + 1
    phases = jnp.mod(freq_index[1][:, None] * odd_time[None, :], 2 * time_count)
    angles = phases.astype(jnp.float32) * (math.pi / time_count)
    cosine = jnp.cos(angles) / math.sqrt(time_count)
    sine_part = jnp.sin(angles) / math.sqrt(time_count)
    real_rows = jnp.stack([cosine, -sine_part], axis=-1)
    imag_rows = jnp.stack([sine_part, cosine], axis=-1)
    return jnp.stack([real_rows, imag_rows], axis=1).astype(jnp.bfloat16)


def batched(left_matrix, right_matrix):
    return jnp.einsum("bij,bjk->bik", left_matrix, right_matrix, preferred_element_type=jnp.float32)


def newton_green(dyson, guess):
    full_shape = dyson.shape
    batch_size = full_shape[0] * full_shape[1]
    matrix_size = full_shape[3]
    flat_dyson = dyson.reshape(batch_size, 2, matrix_size, matrix_size)
    flat_guess = guess.reshape(batch_size, 2, matrix_size, matrix_size)
    dyson_real, dyson_imag = (flat_dyson[:, 0], flat_dyson[:, 1])
    guess_real, guess_imag = (flat_guess[:, 0], flat_guess[:, 1])
    product_real = batched(dyson_real, guess_real) - batched(dyson_imag, guess_imag)
    product_imag = batched(dyson_real, guess_imag) + batched(dyson_imag, guess_real)
    unit_matrix = jnp.eye(matrix_size, dtype=jnp.float32)
    corr_real = (2.0 * unit_matrix - product_real).astype(jnp.bfloat16)
    corr_imag = (-product_imag).astype(jnp.bfloat16)
    green_real = batched(guess_real, corr_real) - batched(guess_imag, corr_imag)
    green_imag = batched(guess_real, corr_imag) + batched(guess_imag, corr_real)
    green_freq = jnp.stack([green_real, green_imag], axis=1).astype(jnp.bfloat16)
    return green_freq.reshape(full_shape)


def to_time(phase_table, values):
    return jnp.einsum("tdwc,wrcse->trdse", phase_table, values, preferred_element_type=jnp.float32)


def to_freq(phase_table, values):
    return jnp.einsum("vdtc,trcse->vrdse", phase_table, values, preferred_element_type=jnp.float32)


def polarize(green_time, hole_time):
    green_real, green_imag = (green_time[:, :, 0], green_time[:, :, 1])
    hole_real, hole_imag = (hole_time[:, :, 0], hole_time[:, :, 1])
    polar_real = green_real * hole_real - green_imag * hole_imag
    polar_imag = green_real * hole_imag + green_imag * hole_real
    return jnp.stack([polar_real, polar_imag], axis=2).astype(jnp.bfloat16)


def screen_block(polar_freq, coulomb):
    screened_polar = jnp.einsum(
        "ij,frcjk->frcik", coulomb, polar_freq, preferred_element_type=jnp.float32
    )
    screened_polar = screened_polar.astype(jnp.bfloat16)
    product = jnp.einsum(
        "frcij,jk->frcik", screened_polar, coulomb, preferred_element_type=jnp.float32
    )
    real_mask = (jnp.arange(2) == 0).astype(jnp.float32)[None, None, :, None, None]
    return (product + real_mask * coulomb.astype(jnp.float32)[None, None, None]).astype(
        jnp.bfloat16
    )


def take_vectors(values, partner):
    return jnp.concatenate(
        [lax.dynamic_slice_in_dim(values, partner[r], 1, axis=1) for r in range(values.shape[1])], axis=1
    )


def local(dyson, guess, coulomb, partner, freq_index):
    green_freq = newton_green(dyson, guess)
    forward = fermion_table(freq_index, NT)
    backward = boson_table(freq_index, NT)
    hole_freq = jnp.swapaxes(take_vectors(green_freq, partner), 3, 4)
    green_part = lax.all_to_all(green_freq, "freq", split_axis=3, concat_axis=0, tiled=True)
    hole_part = lax.all_to_all(hole_freq, "freq", split_axis=3, concat_axis=0, tiled=True)
    green_time = to_time(forward, green_part)
    hole_time = to_time(forward, hole_part)[::-1]
    polar_freq = to_freq(backward, polarize(green_time, hole_time)).astype(jnp.bfloat16)
    return screen_block(
        lax.all_to_all(polar_freq, "freq", split_axis=0, concat_axis=3, tiled=True), coulomb
    )


MESH = pl.DeviceIdType.MESH
PEERS = 16
TILE = 128
HALF = 64
PAIRS = [(0, 1), (0, 2), (0, 3), (1, 2), (1, 3), (2, 3)]
VMEM_LIMIT = 60 * 2**20


def dot(left, right):
    return jnp.dot(left, right, preferred_element_type=jnp.float32)


def greet_all(me):
    barrier = pltpu.get_barrier_semaphore()
    for step in range(1, PEERS):
        peer = lax.rem(me + step, PEERS)
        pl.semaphore_signal(barrier, inc=1, device_id={"freq": peer}, device_id_type=MESH)
    pl.semaphore_wait(barrier, PEERS - 1)


def peer_at(me, step):
    half = PEERS // 2
    side = me // half
    if step < half:
        return (1 - side) * half + lax.rem(me + step, half)
    return side * half + lax.rem(me + step - half + 1, half)


def green_kernel(freqs, vectors, dyson_ref, guess_ref, recv_ref, corr, green, send, send_sem, recv_sem, own_sem):
    me = lax.axis_index("freq")
    grid_step = pl.program_id(0)
    steps = freqs * vectors
    freq, vector = grid_step // vectors, lax.rem(grid_step, vectors)

    def remote(step, source, target):
        return pltpu.make_async_remote_copy(
            src_ref=source,
            dst_ref=target,
            send_sem=send_sem.at[step],
            recv_sem=recv_sem.at[me],
            device_id={"freq": peer_at(me, step)},
            device_id_type=MESH,
        )

    @pl.when(grid_step == 0)
    def _():
        greet_all(me)

    size = dyson_ref.shape[-1]
    guess_real, guess_imag = guess_ref[0, 0, 0], guess_ref[0, 0, 1]
    for row in range(0, size, 256):
        rows = pl.ds(row, 256)
        dyson_real, dyson_imag = dyson_ref[0, 0, 0, rows, :], dyson_ref[0, 0, 1, rows, :]
        line = lax.broadcasted_iota(jnp.int32, (256, size), 0) + row
        column = lax.broadcasted_iota(jnp.int32, (256, size), 1)
        twice = jnp.where(line == column, 2.0, 0.0).astype(jnp.float32)
        product_real = dot(dyson_real, guess_real) - dot(dyson_imag, guess_imag)
        product_imag = dot(dyson_real, guess_imag) + dot(dyson_imag, guess_real)
        corr[0, rows, :] = (twice - product_real).astype(jnp.bfloat16)
        corr[1, rows, :] = (-product_imag).astype(jnp.bfloat16)
    corr_real, corr_imag = corr[0], corr[1]
    for row in range(0, size, 256):
        rows = pl.ds(row, 256)
        left_real, left_imag = guess_ref[0, 0, 0, rows, :], guess_ref[0, 0, 1, rows, :]
        green[0, rows, :] = dot(left_real, corr_real) - dot(left_imag, corr_imag)
        green[1, rows, :] = dot(left_real, corr_imag) + dot(left_imag, corr_real)

    for part in range(2):
        for index, (low, high) in enumerate(PAIRS):
            upper = green[part, pl.ds(low * TILE, TILE), pl.ds(high * TILE, TILE)].astype(jnp.bfloat16)
            lower = green[part, pl.ds(high * TILE, TILE), pl.ds(low * TILE, TILE)].T.astype(jnp.bfloat16)
            for half in range(2):
                cut = slice(half * HALF, (half + 1) * HALF)
                send[freq, vector, 2 * index + half, part, pl.ds(0, HALF), :] = upper[cut]
                send[freq, vector, 2 * index + half, part, pl.ds(HALF, HALF), :] = lower[cut]
        for block in range(4):
            span = pl.ds(block * TILE, TILE)
            send[freq, vector, 2 * len(PAIRS) + block, part] = green[part, span, span].astype(jnp.bfloat16)

    for step in range(PEERS - 1):
        remote(step, send.at[freq, vector, peer_at(me, step)], recv_ref.at[me * freqs + freq, vector]).start()
    pltpu.make_async_copy(send.at[freq, vector, me], recv_ref.at[me * freqs + freq, vector], own_sem).start()

    @pl.when(grid_step == steps - 1)
    def _():
        own_slab = recv_ref.at[pl.ds(me * freqs, freqs)]
        for step in range(PEERS - 1):
            remote(step, send.at[:, :, peer_at(me, step)], own_slab).wait_send()
        pltpu.make_async_copy(send.at[:, :, me], own_slab, own_sem).wait()
        for step in range(PEERS - 1):
            peer = peer_at(me, step)
            slab = recv_ref.at[pl.ds(peer * freqs, freqs)]
            pltpu.make_async_remote_copy(
                src_ref=slab,
                dst_ref=slab,
                send_sem=send_sem.at[step],
                recv_sem=recv_sem.at[peer],
                device_id={"freq": peer},
                device_id_type=MESH,
            ).wait_recv()


def green_blocks(dyson, guess):
    freqs, vectors, _, size, _ = dyson.shape
    steps = freqs * vectors
    block = pl.BlockSpec((1, 1, 2, size, size), lambda g: (g // vectors, g % vectors, 0, 0, 0))
    return pl.pallas_call(
        functools.partial(green_kernel, freqs, vectors),
        out_shape=jax.ShapeDtypeStruct((freqs * PEERS, vectors, 2, TILE, TILE), jnp.bfloat16),
        grid=(steps,),
        in_specs=[block, block],
        out_specs=pl.BlockSpec(memory_space=pl.ANY),
        scratch_shapes=[
            pltpu.VMEM((2, size, size), jnp.bfloat16),
            pltpu.VMEM((2, size, size), jnp.float32),
            pltpu.VMEM((freqs, vectors, PEERS, 2, TILE, TILE), jnp.bfloat16),
            pltpu.SemaphoreType.DMA((PEERS - 1,)),
            pltpu.SemaphoreType.DMA((PEERS,)),
            pltpu.SemaphoreType.DMA,
        ],
        compiler_params=pltpu.CompilerParams(
            collective_id=0, has_side_effects=True, vmem_limit_bytes=VMEM_LIMIT
        ),
    )(dyson, guess)


def mirror_kernel(diagonal_ref, values_ref, out_ref):
    @pl.when(diagonal_ref[0] == 0)
    def _():
        out_ref[:, :, pl.ds(0, HALF), :] = values_ref[:, :, pl.ds(HALF, HALF), :]
        out_ref[:, :, pl.ds(HALF, HALF), :] = values_ref[:, :, pl.ds(0, HALF), :]

    @pl.when(diagonal_ref[0] != 0)
    def _():
        for row in range(values_ref.shape[0]):
            for part in range(2):
                out_ref[row, part] = values_ref[row, part].astype(jnp.float32).T.astype(jnp.bfloat16)


def mirror(diagonal, values):
    freqs, vectors, _, _, _ = values.shape
    flat = values.reshape(freqs * vectors, 2, TILE, TILE)
    block = pl.BlockSpec((32, 2, TILE, TILE), lambda g, flag: (g, 0, 0, 0))
    out = pl.pallas_call(
        mirror_kernel,
        out_shape=jax.ShapeDtypeStruct(flat.shape, flat.dtype),
        grid_spec=pltpu.PrefetchScalarGridSpec(
            num_scalar_prefetch=1, grid=(flat.shape[0] // 32,), in_specs=[block], out_specs=block
        ),
        compiler_params=pltpu.CompilerParams(vmem_limit_bytes=VMEM_LIMIT),
    )(diagonal, flat)
    return out.reshape(values.shape)


CHUNK = 16
GROUP = 4


def polar_kernel(
    partner_ref, green_ref, hole_ref, forward_ref, mirrored_ref, backward_ref, recv_ref,
    green_wide, hole_wide, out_wide, send, send_sem, recv_sem, own_sem,
):
    me = lax.axis_index("freq")
    chunk, vector = pl.program_id(0), pl.program_id(1)
    share = send.shape[2] // PEERS

    def remote(step, source, target):
        return pltpu.make_async_remote_copy(
            src_ref=source,
            dst_ref=target,
            send_sem=send_sem.at[step],
            recv_sem=recv_sem.at[me],
            device_id={"freq": peer_at(me, step)},
            device_id_type=MESH,
        )

    @pl.when((chunk == 0) & (vector == 0))
    def _():
        greet_all(me)

    rows = green_wide.shape[0]
    depth = rows // CHUNK
    green_wide[...] = green_ref[...].reshape(rows, TILE).astype(jnp.float32)
    hole_wide[...] = hole_ref[:, partner_ref[vector]].reshape(rows, TILE).astype(jnp.float32)
    times = forward_ref.shape[0] // 2
    for start in range(0, CHUNK, GROUP):
        def gather(wide):
            return jnp.concatenate(
                [wide[pl.ds(start + k, depth, stride=CHUNK), :] for k in range(GROUP)], axis=1
            ).astype(jnp.bfloat16)
        green_time = dot(forward_ref[...], gather(green_wide))
        hole_time = dot(mirrored_ref[...], gather(hole_wide))
        green_real, green_imag = green_time[:times], green_time[times:]
        hole_real, hole_imag = hole_time[:times], hole_time[times:]
        polar_real = green_real * hole_real - green_imag * hole_imag
        polar_imag = green_real * hole_imag + green_imag * hole_real
        polar = jnp.concatenate([polar_real, polar_imag], axis=0).astype(jnp.bfloat16)
        result = dot(backward_ref[...], polar)
        for k in range(GROUP):
            out_wide[pl.ds(start + k, result.shape[0], stride=CHUNK), :] = result[:, k * TILE:(k + 1) * TILE]
    send[chunk, vector] = out_wide[...].astype(jnp.bfloat16).reshape(send.shape[2:])
    for step in range(PEERS - 1):
        part = pl.ds(peer_at(me, step) * share, share)
        remote(step, send.at[chunk, vector, part], recv_ref.at[me, chunk, vector]).start()
    own = pl.ds(me * share, share)
    pltpu.make_async_copy(send.at[chunk, vector, own], recv_ref.at[me, chunk, vector], own_sem).start()

    @pl.when((chunk == pl.num_programs(0) - 1) & (vector == pl.num_programs(1) - 1))
    def _():
        for step in range(PEERS - 1):
            part = pl.ds(peer_at(me, step) * share, share)
            remote(step, send.at[:, :, part], recv_ref.at[me]).wait_send()
        pltpu.make_async_copy(send.at[:, :, own], recv_ref.at[me], own_sem).wait()
        for step in range(PEERS - 1):
            peer = peer_at(me, step)
            pltpu.make_async_remote_copy(
                src_ref=recv_ref.at[peer],
                dst_ref=recv_ref.at[peer],
                send_sem=send_sem.at[step],
                recv_sem=recv_sem.at[peer],
                device_id={"freq": peer},
                device_id_type=MESH,
            ).wait_recv()


def polarization(partner, green, hole, forward, mirrored, backward):
    freqs, vectors, _, _, _ = green.shape
    outs = backward.shape[0] // 2
    chunks = TILE // CHUNK
    return pl.pallas_call(
        polar_kernel,
        out_shape=jax.ShapeDtypeStruct(
            (PEERS, chunks, vectors, outs // PEERS, 2, CHUNK, TILE), jnp.bfloat16
        ),
        grid=(chunks, vectors),
        in_specs=[
            pl.BlockSpec(memory_space=pltpu.SMEM),
            pl.BlockSpec((freqs, 1, 2, CHUNK, TILE), lambda k, r: (0, r, 0, k, 0)),
            pl.BlockSpec((freqs, vectors, 2, CHUNK, TILE), lambda k, r: (0, 0, 0, k, 0)),
            pl.BlockSpec(forward.shape, lambda k, r: (0, 0)),
            pl.BlockSpec(forward.shape, lambda k, r: (0, 0)),
            pl.BlockSpec(backward.shape, lambda k, r: (0, 0)),
        ],
        out_specs=pl.BlockSpec(memory_space=pl.ANY),
        scratch_shapes=[
            pltpu.VMEM((freqs * 2 * CHUNK, TILE), jnp.float32),
            pltpu.VMEM((freqs * 2 * CHUNK, TILE), jnp.float32),
            pltpu.VMEM((outs * 2 * CHUNK, TILE), jnp.float32),
            pltpu.VMEM((chunks, vectors, outs, 2, CHUNK, TILE), jnp.bfloat16),
            pltpu.SemaphoreType.DMA((PEERS - 1,)),
            pltpu.SemaphoreType.DMA((PEERS,)),
            pltpu.SemaphoreType.DMA,
        ],
        compiler_params=pltpu.CompilerParams(
            collective_id=1, has_side_effects=True, vmem_limit_bytes=VMEM_LIMIT
        ),
    )(partner, green, hole, forward, mirrored, backward)


def screen_kernel(blocks_ref, coulomb_ref, out_ref, polar, mixed):
    chunks = blocks_ref.shape[1]
    mid = chunks // 2

    def rows_of(source, part, start, count):
        return blocks_ref[source, pl.ds(start, count), 0, 0, part].reshape(count * CHUNK, TILE)

    for part in range(2):
        for index, (low, high) in enumerate(PAIRS):
            upper = [rows_of(2 * index + half, part, 0, mid) for half in range(2)]
            lower = [rows_of(2 * index + half, part, mid, mid) for half in range(2)]
            for half in range(2):
                polar[part, pl.ds(low * TILE + half * HALF, HALF), pl.ds(high * TILE, TILE)] = upper[half]
            turned = jnp.concatenate(lower, axis=0).astype(jnp.float32).T.astype(jnp.bfloat16)
            polar[part, pl.ds(high * TILE, TILE), pl.ds(low * TILE, TILE)] = turned
        for block in range(4):
            span = pl.ds(block * TILE, TILE)
            polar[part, span, span] = rows_of(2 * len(PAIRS) + block, part, 0, chunks)
    size = coulomb_ref.shape[0]
    for part in range(2):
        for row in range(0, size, 256):
            rows = pl.ds(row, 256)
            mixed[rows, :] = dot(coulomb_ref[rows, :], polar[part]).astype(jnp.bfloat16)
        for row in range(0, size, 256):
            rows = pl.ds(row, 256)
            product = dot(mixed[rows, :], coulomb_ref[...])
            if part == 0:
                product = product + coulomb_ref[rows, :].astype(jnp.float32)
            out_ref[0, 0, part, rows, :] = product.astype(jnp.bfloat16)


def screen_blocks(blocks, coulomb):
    _, chunks, vectors, freqs, _, _, _ = blocks.shape
    size = coulomb.shape[0]
    return pl.pallas_call(
        screen_kernel,
        out_shape=jax.ShapeDtypeStruct((freqs, vectors, 2, size, size), jnp.bfloat16),
        grid=(freqs, vectors),
        in_specs=[
            pl.BlockSpec((PEERS, chunks, 1, 1, 2, CHUNK, TILE), lambda v, r: (0, 0, r, v, 0, 0, 0)),
            pl.BlockSpec((size, size), lambda v, r: (0, 0)),
        ],
        out_specs=pl.BlockSpec((1, 1, 2, size, size), lambda v, r: (v, r, 0, 0, 0)),
        scratch_shapes=[
            pltpu.VMEM((2, size, size), jnp.bfloat16),
            pltpu.VMEM((size, size), jnp.bfloat16),
        ],
        compiler_params=pltpu.CompilerParams(vmem_limit_bytes=VMEM_LIMIT),
    )(blocks, coulomb)


def tables(freq_index):
    forward = fermion_table(freq_index, NT)
    backward = boson_table(freq_index, NT)
    freqs = forward.shape[2]
    plain = jnp.transpose(forward, (1, 0, 2, 3)).reshape(2 * NT, 2 * freqs)
    mirrored = jnp.transpose(forward[::-1], (1, 0, 2, 3)).reshape(2 * NT, 2 * freqs)
    back = jnp.transpose(backward, (0, 1, 3, 2)).reshape(2 * freqs, 2 * NT)
    return plain, mirrored, back


def local_paired(dyson, guess, coulomb, partner, freq_index):
    forward, mirrored, backward = tables(freq_index)
    diagonal = (lax.axis_index("freq") >= 2 * len(PAIRS)).astype(jnp.int32).reshape(1)
    green = green_blocks(dyson, guess)
    hole = mirror(diagonal, green)
    polar = polarization(partner, green, hole, forward, mirrored, backward)
    return screen_blocks(polar, coulomb)


def solution(mesh):
    in_specs = (
        P(("groups", "freq"), None, None, None, None),
        P(("groups", "freq"), None, None, None, None),
        P("groups", None),
        P(),
        P(),
    )
    out_specs = P(("groups", "freq"), None, None, None, None)
    body = local_paired if mesh.shape["freq"] == PEERS else local
    return jax.shard_map(body, mesh=mesh, in_specs=in_specs, out_specs=out_specs, check_vma=False)
```

```python
import functools
import math

import jax
import jax.numpy as jnp
from jax import lax
from jax.experimental import pallas as pl
from jax.experimental.pallas import tpu as pltpu
from jax.sharding import PartitionSpec as P

NT = 64


def fermion_table(freq_index, time_count):
    freq_count = freq_index.shape[1]
    odd_freq = 2 * freq_index[0] + 1
    odd_time = 2 * jnp.arange(time_count, dtype=jnp.int32) + 1
    phases = jnp.mod(odd_time[:, None] * odd_freq[None, :], 4 * time_count)
    angles = phases.astype(jnp.float32) * (math.pi / (2 * time_count))
    cosine = jnp.cos(angles) / math.sqrt(freq_count)
    sine_part = jnp.sin(angles) / math.sqrt(freq_count)
    real_rows = jnp.stack([cosine, sine_part], axis=-1)
    imag_rows = jnp.stack([-sine_part, cosine], axis=-1)
    return jnp.stack([real_rows, imag_rows], axis=1).astype(jnp.bfloat16)


def boson_table(freq_index, time_count):
    odd_time = 2 * jnp.arange(time_count, dtype=jnp.int32) + 1
    phases = jnp.mod(freq_index[1][:, None] * odd_time[None, :], 2 * time_count)
    angles = phases.astype(jnp.float32) * (math.pi / time_count)
    cosine = jnp.cos(angles) / math.sqrt(time_count)
    sine_part = jnp.sin(angles) / math.sqrt(time_count)
    real_rows = jnp.stack([cosine, -sine_part], axis=-1)
    imag_rows = jnp.stack([sine_part, cosine], axis=-1)
    return jnp.stack([real_rows, imag_rows], axis=1).astype(jnp.bfloat16)


def batched(left_matrix, right_matrix):
    return jnp.einsum("bij,bjk->bik", left_matrix, right_matrix, preferred_element_type=jnp.float32)


def newton_green(dyson, guess):
    full_shape = dyson.shape
    batch_size = full_shape[0] * full_shape[1]
    matrix_size = full_shape[3]
    flat_dyson = dyson.reshape(batch_size, 2, matrix_size, matrix_size)
    flat_guess = guess.reshape(batch_size, 2, matrix_size, matrix_size)
    dyson_real, dyson_imag = (flat_dyson[:, 0], flat_dyson[:, 1])
    guess_real, guess_imag = (flat_guess[:, 0], flat_guess[:, 1])
    product_real = batched(dyson_real, guess_real) - batched(dyson_imag, guess_imag)
    product_imag = batched(dyson_real, guess_imag) + batched(dyson_imag, guess_real)
    unit_matrix = jnp.eye(matrix_size, dtype=jnp.float32)
    corr_real = (2.0 * unit_matrix - product_real).astype(jnp.bfloat16)
    corr_imag = (-product_imag).astype(jnp.bfloat16)
    green_real = batched(guess_real, corr_real) - batched(guess_imag, corr_imag)
    green_imag = batched(guess_real, corr_imag) + batched(guess_imag, corr_real)
    green_freq = jnp.stack([green_real, green_imag], axis=1).astype(jnp.bfloat16)
    return green_freq.reshape(full_shape)


def to_time(phase_table, values):
    return jnp.einsum("tdwc,wrcse->trdse", phase_table, values, preferred_element_type=jnp.float32)


def to_freq(phase_table, values):
    return jnp.einsum("vdtc,trcse->vrdse", phase_table, values, preferred_element_type=jnp.float32)


def polarize(green_time, hole_time):
    green_real, green_imag = (green_time[:, :, 0], green_time[:, :, 1])
    hole_real, hole_imag = (hole_time[:, :, 0], hole_time[:, :, 1])
    polar_real = green_real * hole_real - green_imag * hole_imag
    polar_imag = green_real * hole_imag + green_imag * hole_real
    return jnp.stack([polar_real, polar_imag], axis=2).astype(jnp.bfloat16)


def screen_block(polar_freq, coulomb):
    screened_polar = jnp.einsum(
        "ij,frcjk->frcik", coulomb, polar_freq, preferred_element_type=jnp.float32
    )
    screened_polar = screened_polar.astype(jnp.bfloat16)
    product = jnp.einsum(
        "frcij,jk->frcik", screened_polar, coulomb, preferred_element_type=jnp.float32
    )
    real_mask = (jnp.arange(2) == 0).astype(jnp.float32)[None, None, :, None, None]
    return (product + real_mask * coulomb.astype(jnp.float32)[None, None, None]).astype(
        jnp.bfloat16
    )


def take_vectors(values, partner):
    return jnp.concatenate(
        [lax.dynamic_slice_in_dim(values, partner[r], 1, axis=1) for r in range(values.shape[1])], axis=1
    )


def local(dyson, guess, coulomb, partner, freq_index):
    green_freq = newton_green(dyson, guess)
    forward = fermion_table(freq_index, NT)
    backward = boson_table(freq_index, NT)
    hole_freq = jnp.swapaxes(take_vectors(green_freq, partner), 3, 4)
    green_part = lax.all_to_all(green_freq, "freq", split_axis=3, concat_axis=0, tiled=True)
    hole_part = lax.all_to_all(hole_freq, "freq", split_axis=3, concat_axis=0, tiled=True)
    green_time = to_time(forward, green_part)
    hole_time = to_time(forward, hole_part)[::-1]
    polar_freq = to_freq(backward, polarize(green_time, hole_time)).astype(jnp.bfloat16)
    return screen_block(
        lax.all_to_all(polar_freq, "freq", split_axis=0, concat_axis=3, tiled=True), coulomb
    )


MESH = pl.DeviceIdType.MESH
PEERS = 16
TILE = 128
HALF = 64
PAIRS = [(0, 1), (0, 2), (0, 3), (1, 2), (1, 3), (2, 3)]
VMEM_LIMIT = 60 * 2**20
CHUNK = 16
CHUNKS = HALF // CHUNK
GROUP = 4


def dot(left, right):
    return jnp.dot(left, right, preferred_element_type=jnp.float32)


def greet_all(me):
    barrier = pltpu.get_barrier_semaphore()
    for step in range(1, PEERS):
        peer = lax.rem(me + step, PEERS)
        pl.semaphore_signal(barrier, inc=1, device_id={"freq": peer}, device_id_type=MESH)
    pl.semaphore_wait(barrier, PEERS - 1)


def peer_at(me, step):
    half = PEERS // 2
    side = me // half
    if step < half:
        return (1 - side) * half + lax.rem(me + step, half)
    return side * half + lax.rem(me + step - half + 1, half)


def remote_copy(source, target, send_sem, recv_sem, peer):
    return pltpu.make_async_remote_copy(
        src_ref=source,
        dst_ref=target,
        send_sem=send_sem,
        recv_sem=recv_sem,
        device_id={"freq": peer},
        device_id_type=MESH,
    )


def newton_step(dyson_ref, guess_ref, corr, green):
    size = dyson_ref.shape[-1]
    guess_real, guess_imag = guess_ref[0, 0, 0], guess_ref[0, 0, 1]
    for row in range(0, size, 256):
        rows = pl.ds(row, 256)
        dyson_real, dyson_imag = dyson_ref[0, 0, 0, rows, :], dyson_ref[0, 0, 1, rows, :]
        line = lax.broadcasted_iota(jnp.int32, (256, size), 0) + row
        column = lax.broadcasted_iota(jnp.int32, (256, size), 1)
        twice = jnp.where(line == column, 2.0, 0.0).astype(jnp.float32)
        product_real = dot(dyson_real, guess_real) - dot(dyson_imag, guess_imag)
        product_imag = dot(dyson_real, guess_imag) + dot(dyson_imag, guess_real)
        corr[0, rows, :] = (twice - product_real).astype(jnp.bfloat16)
        corr[1, rows, :] = (-product_imag).astype(jnp.bfloat16)
    corr_real, corr_imag = corr[0], corr[1]
    for row in range(0, size, 256):
        rows = pl.ds(row, 256)
        left_real, left_imag = guess_ref[0, 0, 0, rows, :], guess_ref[0, 0, 1, rows, :]
        green[0, rows, :] = dot(left_real, corr_real) - dot(left_imag, corr_imag)
        green[1, rows, :] = dot(left_real, corr_imag) + dot(left_imag, corr_real)


def fold_indices():
    line = lax.broadcasted_iota(jnp.int32, (HALF, TILE), 0)
    column = lax.broadcasted_iota(jnp.int32, (HALF, TILE), 1)
    return line, column


def pack_step(green, send, freqs, freq, vector):
    line, column = fold_indices()

    def put(peer, part, side, values):
        values = values.astype(jnp.bfloat16)
        for chunk in range(CHUNKS):
            send[chunk, peer * freqs + freq, vector, part, side] = values[chunk * CHUNK:(chunk + 1) * CHUNK]

    for part in range(2):
        for index, (low, high) in enumerate(PAIRS):
            upper = green[part, pl.ds(low * TILE, TILE), pl.ds(high * TILE, TILE)]
            lower = green[part, pl.ds(high * TILE, TILE), pl.ds(low * TILE, TILE)].T
            for half in range(2):
                cut = slice(half * HALF, (half + 1) * HALF)
                put(2 * index + half, part, 0, upper[cut])
                put(2 * index + half, part, 1, lower[cut])
        for block in range(4):
            span = pl.ds(block * TILE, TILE)
            plain = green[part, span, span]
            turned = plain.T
            plain_low = pltpu.roll(plain[HALF:], HALF, 1)
            turned_low = pltpu.roll(turned[HALF:], HALF, 1)
            put(2 * len(PAIRS) + block, part, 0, jnp.where(column >= line, plain[:HALF], plain_low))
            put(
                2 * len(PAIRS) + block, part, 1,
                jnp.where(column > line, turned[:HALF], jnp.where(column == line, plain_low, turned_low)),
            )


def polar_chunk(chunk, me, partner_ref, forward_ref, backward_ref, held, wide, timed, send):
    freqs, vectors = held.shape[0], held.shape[1]
    depth = 2 * freqs
    times = backward_ref.shape[1] // 2
    lanes = GROUP * TILE
    stride = 2 * CHUNK

    def widen(vector, carry):
        wide[vector] = held[:, vector].reshape(depth * stride, TILE).astype(jnp.float32)
        return carry

    lax.fori_loop(0, vectors, widen, 0)
    for start in range(0, CHUNK, GROUP):

        def transform(vector, carry):
            gathered = jnp.concatenate(
                [
                    wide[vector, pl.ds(side * CHUNK + start + k, depth, stride=stride), :]
                    for side in range(2)
                    for k in range(GROUP)
                ],
                axis=1,
            ).astype(jnp.bfloat16)
            timed[vector] = dot(forward_ref[...], gathered)
            return carry

        def product(vector, carry):
            other = partner_ref[vector]
            lane = lax.broadcasted_iota(jnp.int32, (times, lanes), 1)
            itself = (lax.rem(lane, TILE) == lax.div(lane, TILE) + chunk * CHUNK + start) & (me >= 2 * len(PAIRS))
            parts = []
            for side in range(2):
                here, there = pl.ds(side * lanes, lanes), pl.ds((1 - side) * lanes, lanes)
                green_real = timed[vector, pl.ds(0, times), here]
                green_imag = timed[vector, pl.ds(times, times), here]
                hole_real = jnp.where(
                    itself, timed[other, pl.ds(2 * times, times), here], timed[other, pl.ds(2 * times, times), there]
                )
                hole_imag = jnp.where(
                    itself, timed[other, pl.ds(3 * times, times), here], timed[other, pl.ds(3 * times, times), there]
                )
                parts.append(
                    jnp.concatenate(
                        [
                            green_real * hole_real - green_imag * hole_imag,
                            green_real * hole_imag + green_imag * hole_real,
                        ],
                        axis=0,
                    ).astype(jnp.bfloat16)
                )
            for side in range(2):
                result = dot(backward_ref[...], parts[side])
                for k in range(GROUP):
                    wide[vector, pl.ds(side * CHUNK + start + k, result.shape[0], stride=stride), :] = result[
                        :, k * TILE:(k + 1) * TILE
                    ]
            return carry

        lax.fori_loop(0, vectors, transform, 0)
        lax.fori_loop(0, vectors, product, 0)

    def narrow(vector, carry):
        send[chunk, :, vector] = wide[vector].astype(jnp.bfloat16).reshape(freqs, 2, 2, CHUNK, TILE)
        return carry

    lax.fori_loop(0, vectors, narrow, 0)


def exchange_kernel(
    freqs, vectors, partner_ref, forward_ref, backward_ref, dyson_ref, guess_ref, first_ref, second_ref,
    corr, green, send, held, wide, timed,
    send_first, recv_first, own_first, send_second, recv_second, own_second, load_sem,
):
    me = lax.axis_index("freq")
    grid_step = pl.program_id(0)
    steps = freqs * vectors
    freq, vector = grid_step // vectors, lax.rem(grid_step, vectors)
    mine = pl.ds(me * freqs, freqs)

    @pl.when(grid_step == 0)
    def _():
        greet_all(me)

    newton_step(dyson_ref, guess_ref, corr, green)
    pack_step(green, send, freqs, freq, vector)
    for step in range(PEERS - 1):
        peer = peer_at(me, step)
        remote_copy(
            send.at[0, peer * freqs + freq, vector], first_ref.at[0, me * freqs + freq, vector],
            send_first.at[0, step], recv_first.at[0, me], peer,
        ).start()
    pltpu.make_async_copy(
        send.at[0, me * freqs + freq, vector], first_ref.at[0, me * freqs + freq, vector], own_first.at[0]
    ).start()

    @pl.when(grid_step == steps - 1)
    def _():
        def send_later(chunk, carry):
            for step in range(PEERS - 1):
                peer = peer_at(me, step)
                remote_copy(
                    send.at[chunk, pl.ds(peer * freqs, freqs)], first_ref.at[chunk, mine],
                    send_first.at[chunk, step], recv_first.at[chunk, me], peer,
                ).start()
            pltpu.make_async_copy(send.at[chunk, mine], first_ref.at[chunk, mine], own_first.at[chunk]).start()
            return carry

        lax.fori_loop(1, CHUNKS, send_later, 0)

        def middle(chunk, carry):
            for step in range(PEERS - 1):
                peer = peer_at(me, step)
                theirs = pl.ds(peer * freqs, freqs)
                remote_copy(
                    send.at[chunk, theirs], first_ref.at[chunk, theirs],
                    send_first.at[chunk, step], recv_first.at[chunk, peer], peer,
                ).wait()
            pltpu.make_async_copy(send.at[chunk, mine], first_ref.at[chunk, mine], own_first.at[chunk]).wait()
            load = pltpu.make_async_copy(first_ref.at[chunk], held, load_sem)
            load.start()
            load.wait()
            polar_chunk(chunk, me, partner_ref, forward_ref, backward_ref, held, wide, timed, send)

            def send_back(vector, inner):
                for step in range(PEERS - 1):
                    peer = peer_at(me, step)
                    remote_copy(
                        send.at[chunk, pl.ds(peer * freqs, freqs), vector], second_ref.at[me, chunk, :, vector],
                        send_second.at[step], recv_second.at[vector, me], peer,
                    ).start()
                pltpu.make_async_copy(
                    send.at[chunk, mine, vector], second_ref.at[me, chunk, :, vector], own_second.at[vector]
                ).start()
                return inner

            lax.fori_loop(0, vectors, send_back, 0)
            return carry

        lax.fori_loop(0, CHUNKS, middle, 0)

        def arrive(vector, carry):
            for step in range(PEERS - 1):
                peer = peer_at(me, step)
                slab = second_ref.at[peer, :, :, vector]
                remote_copy(slab, slab, send_second.at[step], recv_second.at[vector, peer], peer).wait_recv()
            pltpu.make_async_copy(
                send.at[:, mine, vector], second_ref.at[me, :, :, vector], own_second.at[vector]
            ).wait()
            return carry

        lax.fori_loop(0, vectors, arrive, 0)
        for step in range(PEERS - 1):
            peer = peer_at(me, step)
            remote_copy(
                send.at[:, pl.ds(peer * freqs, freqs)], second_ref.at[me], send_second.at[step],
                recv_second.at[0, me], peer,
            ).wait_send()


def exchange(partner, dyson, guess, forward, backward):
    freqs, vectors, _, size, _ = dyson.shape
    whole = freqs * PEERS
    block = pl.BlockSpec((1, 1, 2, size, size), lambda g: (g // vectors, g % vectors, 0, 0, 0))
    share = (2, 2, CHUNK, TILE)
    return pl.pallas_call(
        functools.partial(exchange_kernel, freqs, vectors),
        out_shape=[
            jax.ShapeDtypeStruct((CHUNKS, whole, vectors) + share, jnp.bfloat16),
            jax.ShapeDtypeStruct((PEERS, CHUNKS, freqs, vectors) + share, jnp.bfloat16),
        ],
        grid=(freqs * vectors,),
        in_specs=[
            pl.BlockSpec(memory_space=pltpu.SMEM),
            pl.BlockSpec(forward.shape, lambda g: (0, 0)),
            pl.BlockSpec(backward.shape, lambda g: (0, 0)),
            block,
            block,
        ],
        out_specs=[pl.BlockSpec(memory_space=pl.ANY)] * 2,
        scratch_shapes=[
            pltpu.VMEM((2, size, size), jnp.bfloat16),
            pltpu.VMEM((2, size, size), jnp.float32),
            pltpu.VMEM((CHUNKS, whole, vectors) + share, jnp.bfloat16),
            pltpu.VMEM((whole, vectors) + share, jnp.bfloat16),
            pltpu.VMEM((vectors, whole * 2 * 2 * CHUNK, TILE), jnp.float32),
            pltpu.VMEM((vectors, forward.shape[0], 2 * GROUP * TILE), jnp.float32),
            pltpu.SemaphoreType.DMA((CHUNKS, PEERS - 1)),
            pltpu.SemaphoreType.DMA((CHUNKS, PEERS)),
            pltpu.SemaphoreType.DMA((CHUNKS,)),
            pltpu.SemaphoreType.DMA((PEERS - 1,)),
            pltpu.SemaphoreType.DMA((vectors, PEERS)),
            pltpu.SemaphoreType.DMA((vectors,)),
            pltpu.SemaphoreType.DMA,
        ],
        compiler_params=pltpu.CompilerParams(
            collective_id=0, has_side_effects=True, vmem_limit_bytes=VMEM_LIMIT
        ),
    )(partner, forward, backward, dyson, guess)


def assemble(rows_of, polar):
    line, column = fold_indices()
    for part in range(2):
        for index, (low, high) in enumerate(PAIRS):
            for half in range(2):
                polar[part, pl.ds(low * TILE + half * HALF, HALF), pl.ds(high * TILE, TILE)] = rows_of(
                    2 * index + half, part, 0
                )
            lower = jnp.concatenate([rows_of(2 * index + half, part, 1) for half in range(2)], axis=0)
            polar[part, pl.ds(high * TILE, TILE), pl.ds(low * TILE, TILE)] = (
                lower.astype(jnp.float32).T.astype(jnp.bfloat16)
            )
        for block in range(4):
            plain = rows_of(2 * len(PAIRS) + block, part, 0).astype(jnp.float32)
            mirrored = rows_of(2 * len(PAIRS) + block, part, 1).astype(jnp.float32)
            turned = jnp.concatenate([mirrored, mirrored], axis=0).T
            top = jnp.where(column >= line, plain, turned[:HALF])
            corner = column - HALF
            bottom = jnp.where(
                corner < 0,
                turned[HALF:],
                jnp.where(
                    corner < line,
                    pltpu.roll(plain, HALF, 1),
                    jnp.where(corner == line, pltpu.roll(mirrored, HALF, 1), turned[:HALF]),
                ),
            )
            span = pl.ds(block * TILE, TILE)
            polar[part, span, span] = jnp.concatenate([top, bottom], axis=0).astype(jnp.bfloat16)


def screen_kernel(blocks_ref, coulomb_ref, out_ref, polar, mixed):
    assemble(lambda peer, part, side: blocks_ref[peer, :, 0, 0, part, side].reshape(HALF, TILE), polar)
    size = coulomb_ref.shape[0]
    for part in range(2):
        for row in range(0, size, 256):
            rows = pl.ds(row, 256)
            mixed[rows, :] = dot(coulomb_ref[rows, :], polar[part]).astype(jnp.bfloat16)
        for row in range(0, size, 256):
            rows = pl.ds(row, 256)
            product = dot(mixed[rows, :], coulomb_ref[...])
            if part == 0:
                product = product + coulomb_ref[rows, :].astype(jnp.float32)
            out_ref[0, 0, part, rows, :] = product.astype(jnp.bfloat16)


def screen_blocks(blocks, coulomb):
    _, _, freqs, vectors, _, _, _, _ = blocks.shape
    size = coulomb.shape[0]
    return pl.pallas_call(
        screen_kernel,
        out_shape=jax.ShapeDtypeStruct((freqs, vectors, 2, size, size), jnp.bfloat16),
        grid=(freqs, vectors),
        in_specs=[
            pl.BlockSpec((PEERS, CHUNKS, 1, 1, 2, 2, CHUNK, TILE), lambda v, r: (0, 0, v, r, 0, 0, 0, 0)),
            pl.BlockSpec((size, size), lambda v, r: (0, 0)),
        ],
        out_specs=pl.BlockSpec((1, 1, 2, size, size), lambda v, r: (v, r, 0, 0, 0)),
        scratch_shapes=[
            pltpu.VMEM((2, size, size), jnp.bfloat16),
            pltpu.VMEM((size, size), jnp.bfloat16),
        ],
        compiler_params=pltpu.CompilerParams(vmem_limit_bytes=VMEM_LIMIT),
    )(blocks, coulomb)


def tables(freq_index):
    forward = fermion_table(freq_index, NT)
    backward = boson_table(freq_index, NT)
    freqs = forward.shape[2]
    plain = jnp.transpose(forward, (1, 0, 2, 3)).reshape(2 * NT, 2 * freqs)
    mirrored = jnp.transpose(forward[::-1], (1, 0, 2, 3)).reshape(2 * NT, 2 * freqs)
    back = jnp.transpose(backward, (0, 1, 3, 2)).reshape(2 * freqs, 2 * NT)
    return plain, mirrored, back


def local_paired(dyson, guess, coulomb, partner, freq_index):
    forward, mirrored, backward = tables(freq_index)
    _, polar = exchange(partner, dyson, guess, jnp.concatenate([forward, mirrored], axis=0), backward)
    return screen_blocks(polar, coulomb)


def solution(mesh):
    in_specs = (
        P(("groups", "freq"), None, None, None, None),
        P(("groups", "freq"), None, None, None, None),
        P("groups", None),
        P(),
        P(),
    )
    out_specs = P(("groups", "freq"), None, None, None, None)
    body = local_paired if mesh.shape["freq"] == PEERS else local
    return jax.shard_map(body, mesh=mesh, in_specs=in_specs, out_specs=out_specs, check_vma=False)
```

```python
import functools
import math

import jax
import jax.numpy as jnp
from jax import lax
from jax.experimental import pallas as pl
from jax.experimental.pallas import tpu as pltpu
from jax.sharding import PartitionSpec as P

NT = 64


def fermion_table(freq_index, time_count):
    freq_count = freq_index.shape[1]
    odd_freq = 2 * freq_index[0] + 1
    odd_time = 2 * jnp.arange(time_count, dtype=jnp.int32) + 1
    phases = jnp.mod(odd_time[:, None] * odd_freq[None, :], 4 * time_count)
    angles = phases.astype(jnp.float32) * (math.pi / (2 * time_count))
    cosine = jnp.cos(angles) / math.sqrt(freq_count)
    sine_part = jnp.sin(angles) / math.sqrt(freq_count)
    real_rows = jnp.stack([cosine, sine_part], axis=-1)
    imag_rows = jnp.stack([-sine_part, cosine], axis=-1)
    return jnp.stack([real_rows, imag_rows], axis=1).astype(jnp.bfloat16)


def boson_table(freq_index, time_count):
    odd_time = 2 * jnp.arange(time_count, dtype=jnp.int32) + 1
    phases = jnp.mod(freq_index[1][:, None] * odd_time[None, :], 2 * time_count)
    angles = phases.astype(jnp.float32) * (math.pi / time_count)
    cosine = jnp.cos(angles) / math.sqrt(time_count)
    sine_part = jnp.sin(angles) / math.sqrt(time_count)
    real_rows = jnp.stack([cosine, -sine_part], axis=-1)
    imag_rows = jnp.stack([sine_part, cosine], axis=-1)
    return jnp.stack([real_rows, imag_rows], axis=1).astype(jnp.bfloat16)


def batched(left_matrix, right_matrix):
    return jnp.einsum("bij,bjk->bik", left_matrix, right_matrix, preferred_element_type=jnp.float32)


def newton_green(dyson, guess):
    full_shape = dyson.shape
    batch_size = full_shape[0] * full_shape[1]
    matrix_size = full_shape[3]
    flat_dyson = dyson.reshape(batch_size, 2, matrix_size, matrix_size)
    flat_guess = guess.reshape(batch_size, 2, matrix_size, matrix_size)
    dyson_real, dyson_imag = (flat_dyson[:, 0], flat_dyson[:, 1])
    guess_real, guess_imag = (flat_guess[:, 0], flat_guess[:, 1])
    product_real = batched(dyson_real, guess_real) - batched(dyson_imag, guess_imag)
    product_imag = batched(dyson_real, guess_imag) + batched(dyson_imag, guess_real)
    unit_matrix = jnp.eye(matrix_size, dtype=jnp.float32)
    corr_real = (2.0 * unit_matrix - product_real).astype(jnp.bfloat16)
    corr_imag = (-product_imag).astype(jnp.bfloat16)
    green_real = batched(guess_real, corr_real) - batched(guess_imag, corr_imag)
    green_imag = batched(guess_real, corr_imag) + batched(guess_imag, corr_real)
    green_freq = jnp.stack([green_real, green_imag], axis=1).astype(jnp.bfloat16)
    return green_freq.reshape(full_shape)


def to_time(phase_table, values):
    return jnp.einsum("tdwc,wrcse->trdse", phase_table, values, preferred_element_type=jnp.float32)


def to_freq(phase_table, values):
    return jnp.einsum("vdtc,trcse->vrdse", phase_table, values, preferred_element_type=jnp.float32)


def polarize(green_time, hole_time):
    green_real, green_imag = (green_time[:, :, 0], green_time[:, :, 1])
    hole_real, hole_imag = (hole_time[:, :, 0], hole_time[:, :, 1])
    polar_real = green_real * hole_real - green_imag * hole_imag
    polar_imag = green_real * hole_imag + green_imag * hole_real
    return jnp.stack([polar_real, polar_imag], axis=2).astype(jnp.bfloat16)


def screen_block(polar_freq, coulomb):
    screened_polar = jnp.einsum(
        "ij,frcjk->frcik", coulomb, polar_freq, preferred_element_type=jnp.float32
    )
    screened_polar = screened_polar.astype(jnp.bfloat16)
    product = jnp.einsum(
        "frcij,jk->frcik", screened_polar, coulomb, preferred_element_type=jnp.float32
    )
    real_mask = (jnp.arange(2) == 0).astype(jnp.float32)[None, None, :, None, None]
    return (product + real_mask * coulomb.astype(jnp.float32)[None, None, None]).astype(
        jnp.bfloat16
    )


def take_vectors(values, partner):
    return jnp.concatenate(
        [lax.dynamic_slice_in_dim(values, partner[r], 1, axis=1) for r in range(values.shape[1])], axis=1
    )


def local(dyson, guess, coulomb, partner, freq_index):
    green_freq = newton_green(dyson, guess)
    forward = fermion_table(freq_index, NT)
    backward = boson_table(freq_index, NT)
    hole_freq = jnp.swapaxes(take_vectors(green_freq, partner), 3, 4)
    green_part = lax.all_to_all(green_freq, "freq", split_axis=3, concat_axis=0, tiled=True)
    hole_part = lax.all_to_all(hole_freq, "freq", split_axis=3, concat_axis=0, tiled=True)
    green_time = to_time(forward, green_part)
    hole_time = to_time(forward, hole_part)[::-1]
    polar_freq = to_freq(backward, polarize(green_time, hole_time)).astype(jnp.bfloat16)
    return screen_block(
        lax.all_to_all(polar_freq, "freq", split_axis=0, concat_axis=3, tiled=True), coulomb
    )


MESH = pl.DeviceIdType.MESH
PEERS = 16
TILE = 128
HALF = 64
PAIRS = [(0, 1), (0, 2), (0, 3), (1, 2), (1, 3), (2, 3)]
VMEM_LIMIT = 40 * 2**20
EXCHANGE_LIMIT = 46 * 2**20
CHUNK = 16
CHUNKS = HALF // CHUNK
GROUP = 4


def dot(left, right):
    return jnp.dot(left, right, preferred_element_type=jnp.float32)


def greet_all(me):
    barrier = pltpu.get_barrier_semaphore()
    for step in range(1, PEERS):
        peer = lax.rem(me + step, PEERS)
        pl.semaphore_signal(barrier, inc=1, device_id={"freq": peer}, device_id_type=MESH)


def await_greetings():
    pl.semaphore_wait(pltpu.get_barrier_semaphore(), PEERS - 1)


def peer_at(me, step):
    layer, place = me // 4, lax.rem(me, 4)
    side = layer // 2
    if step < 8:
        turn = step // 2
        if step % 2 == 0:
            return 12 * (1 - side) + lax.rem(place + turn, 4)
        return 8 - 4 * side + lax.rem(place + turn, 4)
    turn = step % 4
    if step < 12:
        return 4 * (layer + 1 - 2 * lax.rem(layer, 2)) + lax.rem(place + turn, 4)
    return 4 * layer + lax.rem(place + turn + 1, 4)


def remote_copy(source, target, send_sem, recv_sem, peer):
    return pltpu.make_async_remote_copy(
        src_ref=source,
        dst_ref=target,
        send_sem=send_sem,
        recv_sem=recv_sem,
        device_id={"freq": peer},
        device_id_type=MESH,
    )


def newton_step(dyson_ref, guess_ref, corr, green):
    size = dyson_ref.shape[-1]
    guess_real, guess_imag = guess_ref[0, 0, 0], guess_ref[0, 0, 1]
    for row in range(0, size, 256):
        rows = pl.ds(row, 256)
        dyson_real, dyson_imag = dyson_ref[0, 0, 0, rows, :], dyson_ref[0, 0, 1, rows, :]
        line = lax.broadcasted_iota(jnp.int32, (256, size), 0) + row
        column = lax.broadcasted_iota(jnp.int32, (256, size), 1)
        twice = jnp.where(line == column, 2.0, 0.0).astype(jnp.float32)
        product_real = dot(dyson_real, guess_real) - dot(dyson_imag, guess_imag)
        product_imag = dot(dyson_real, guess_imag) + dot(dyson_imag, guess_real)
        corr[0, rows, :] = (twice - product_real).astype(jnp.bfloat16)
        corr[1, rows, :] = (-product_imag).astype(jnp.bfloat16)
    corr_real, corr_imag = corr[0], corr[1]
    for row in range(0, size, 256):
        rows = pl.ds(row, 256)
        left_real, left_imag = guess_ref[0, 0, 0, rows, :], guess_ref[0, 0, 1, rows, :]
        green[0, rows, :] = dot(left_real, corr_real) - dot(left_imag, corr_imag)
        green[1, rows, :] = dot(left_real, corr_imag) + dot(left_imag, corr_real)


def fold_indices():
    line = lax.broadcasted_iota(jnp.int32, (HALF, TILE), 0)
    column = lax.broadcasted_iota(jnp.int32, (HALF, TILE), 1)
    return line, column


def pack_step(green, send, freqs, freq, vector):
    line, column = fold_indices()

    def put(peer, part, side, values):
        values = values.astype(jnp.bfloat16)
        for chunk in range(CHUNKS):
            send[chunk, peer * freqs + freq, vector, part, side] = values[chunk * CHUNK:(chunk + 1) * CHUNK]

    for part in range(2):
        for index, (low, high) in enumerate(PAIRS):
            upper = green[part, pl.ds(low * TILE, TILE), pl.ds(high * TILE, TILE)]
            lower = green[part, pl.ds(high * TILE, TILE), pl.ds(low * TILE, TILE)].T
            for half in range(2):
                cut = slice(half * HALF, (half + 1) * HALF)
                put(2 * index + half, part, 0, upper[cut])
                put(2 * index + half, part, 1, lower[cut])
        for block in range(4):
            span = pl.ds(block * TILE, TILE)
            plain = green[part, span, span]
            turned = plain.T
            plain_low = pltpu.roll(plain[HALF:], HALF, 1)
            turned_low = pltpu.roll(turned[HALF:], HALF, 1)
            put(2 * len(PAIRS) + block, part, 0, jnp.where(column >= line, plain[:HALF], plain_low))
            put(
                2 * len(PAIRS) + block, part, 1,
                jnp.where(column > line, turned[:HALF], jnp.where(column == line, plain_low, turned_low)),
            )


def fill_tables(index_ref, forward_ref, backward_ref):
    freqs = index_ref.shape[1]
    count = 2 * freqs
    doubled = jnp.concatenate([index_ref[...], index_ref[...]], axis=1)

    def waves(odd_time, freq, steps):
        angles = jnp.bitwise_and(odd_time * freq, 2 * steps - 1).astype(jnp.float32) * (math.pi / steps)
        return jnp.cos(angles), jnp.sin(angles)

    line = lax.broadcasted_iota(jnp.int32, (4 * NT, count), 0)
    column = lax.broadcasted_iota(jnp.int32, (4 * NT, count), 1)
    time = lax.rem(line, NT)
    odd_time = 2 * jnp.where(line < 2 * NT, time, NT - 1 - time) + 1
    cosine, sine_part = waves(odd_time, 2 * doubled[0:1] + 1, 2 * NT)
    imag_row, imag_column = lax.rem(line, 2 * NT) >= NT, column >= freqs
    value = jnp.where(imag_row == imag_column, cosine, jnp.where(imag_row, -sine_part, sine_part))
    forward_ref[...] = (value / math.sqrt(freqs)).astype(jnp.bfloat16)

    line = lax.broadcasted_iota(jnp.int32, (2 * NT, count), 0)
    column = lax.broadcasted_iota(jnp.int32, (2 * NT, count), 1)
    cosine, sine_part = waves(2 * lax.rem(line, NT) + 1, doubled[1:2], NT)
    imag_row, imag_column = line >= NT, column >= freqs
    value = jnp.where(imag_row == imag_column, cosine, jnp.where(imag_row, -sine_part, sine_part))
    backward_ref[...] = (value / math.sqrt(NT)).T.astype(jnp.bfloat16)


def polar_chunk(chunk, me, partner_ref, forward_ref, backward_ref, held, wide, timed, send):
    freqs, vectors = held.shape[0], held.shape[1]
    times = backward_ref.shape[1] // 2
    lanes = GROUP * TILE
    stride = 4 * CHUNK

    def widen(vector, carry):
        wide[vector] = held[:, vector].reshape(freqs * stride, TILE).astype(jnp.float32)
        return carry

    lax.fori_loop(0, vectors, widen, 0)
    for start in range(0, CHUNK, GROUP):

        def transform(vector, carry):
            gathered = jnp.concatenate(
                [
                    jnp.concatenate(
                        [
                            wide[vector, pl.ds((2 * part + side) * CHUNK + start + k, freqs, stride=stride), :]
                            for side in range(2)
                            for k in range(GROUP)
                        ],
                        axis=1,
                    )
                    for part in range(2)
                ],
                axis=0,
            ).astype(jnp.bfloat16)
            timed[vector] = dot(forward_ref[...], gathered)
            return carry

        def product(vector, carry):
            other = partner_ref[vector]
            lane = lax.broadcasted_iota(jnp.int32, (times, lanes), 1)
            itself = (lax.rem(lane, TILE) == lax.div(lane, TILE) + chunk * CHUNK + start) & (me >= 2 * len(PAIRS))
            parts = []
            for side in range(2):
                here, there = pl.ds(side * lanes, lanes), pl.ds((1 - side) * lanes, lanes)
                green_real = timed[vector, pl.ds(0, times), here]
                green_imag = timed[vector, pl.ds(times, times), here]
                hole_real = jnp.where(
                    itself, timed[other, pl.ds(2 * times, times), here], timed[other, pl.ds(2 * times, times), there]
                )
                hole_imag = jnp.where(
                    itself, timed[other, pl.ds(3 * times, times), here], timed[other, pl.ds(3 * times, times), there]
                )
                parts.append(
                    jnp.concatenate(
                        [
                            green_real * hole_real - green_imag * hole_imag,
                            green_real * hole_imag + green_imag * hole_real,
                        ],
                        axis=0,
                    ).astype(jnp.bfloat16)
                )
            for side in range(2):
                result = dot(backward_ref[...], parts[side])
                for part in range(2):
                    for k in range(GROUP):
                        wide[vector, pl.ds((2 * part + side) * CHUNK + start + k, freqs, stride=stride), :] = result[
                            part * freqs:(part + 1) * freqs, k * TILE:(k + 1) * TILE
                        ]
            return carry

        lax.fori_loop(0, vectors, transform, 0)
        lax.fori_loop(0, vectors, product, 0)

    def narrow(vector, carry):
        send[chunk, :, vector] = wide[vector].astype(jnp.bfloat16).reshape(freqs, 2, 2, CHUNK, TILE)
        return carry

    lax.fori_loop(0, vectors, narrow, 0)


def exchange_kernel(
    freqs, vectors, partner_ref, index_ref, coulomb_ref, dyson_ref, guess_ref,
    first_ref, second_ref, early_ref,
    corr, green, send, held, wide, timed, forward_ref, backward_ref, mixed,
    send_first, recv_first, own_first, send_second, recv_second, own_second, load_sem,
):
    me = lax.axis_index("freq")
    grid_step = pl.program_id(0)
    steps = freqs * vectors
    freq, vector = grid_step // vectors, lax.rem(grid_step, vectors)
    mine = pl.ds(me * freqs, freqs)

    @pl.when(grid_step == 0)
    def _():
        greet_all(me)

    newton_step(dyson_ref, guess_ref, corr, green)
    pack_step(green, send, freqs, freq, vector)

    @pl.when(grid_step == 0)
    def _():
        await_greetings()

    for step in range(PEERS - 1):
        peer = peer_at(me, step)
        remote_copy(
            send.at[0, peer * freqs + freq, vector], first_ref.at[0, me * freqs + freq, vector],
            send_first.at[0, step], recv_first.at[0, me], peer,
        ).start()
    pltpu.make_async_copy(
        send.at[0, me * freqs + freq, vector], first_ref.at[0, me * freqs + freq, vector], own_first.at[0]
    ).start()

    @pl.when(grid_step == steps - 1)
    def _():
        def send_later(chunk, carry):
            for step in range(PEERS - 1):
                peer = peer_at(me, step)
                remote_copy(
                    send.at[chunk, pl.ds(peer * freqs, freqs)], first_ref.at[chunk, mine],
                    send_first.at[chunk, step], recv_first.at[chunk, me], peer,
                ).start()
            pltpu.make_async_copy(send.at[chunk, mine], first_ref.at[chunk, mine], own_first.at[chunk]).start()
            return carry

        lax.fori_loop(1, CHUNKS, send_later, 0)
        fill_tables(index_ref, forward_ref, backward_ref)

        def middle(chunk, carry):
            for step in range(PEERS - 1):
                peer = peer_at(me, step)
                theirs = pl.ds(peer * freqs, freqs)
                remote_copy(
                    send.at[chunk, theirs], first_ref.at[chunk, theirs],
                    send_first.at[chunk, step], recv_first.at[chunk, peer], peer,
                ).wait()
            pltpu.make_async_copy(send.at[chunk, mine], first_ref.at[chunk, mine], own_first.at[chunk]).wait()
            load = pltpu.make_async_copy(first_ref.at[chunk], held, load_sem)
            load.start()
            load.wait()
            polar_chunk(chunk, me, partner_ref, forward_ref, backward_ref, held, wide, timed, send)

            def send_back(vector, inner):
                for step in range(PEERS - 1):
                    peer = peer_at(me, step)
                    remote_copy(
                        send.at[chunk, pl.ds(peer * freqs, freqs), vector], second_ref.at[me, chunk, :, vector],
                        send_second.at[step], recv_second.at[vector, me], peer,
                    ).start()
                pltpu.make_async_copy(
                    send.at[chunk, mine, vector], second_ref.at[me, chunk, :, vector], own_second.at[vector]
                ).start()
                return inner

            lax.fori_loop(0, vectors, send_back, 0)
            return carry

        lax.fori_loop(0, CHUNKS, middle, 0)

        def arrive(vector):
            for step in range(PEERS - 1):
                peer = peer_at(me, step)
                slab = second_ref.at[peer, :, :, vector]
                remote_copy(slab, slab, send_second.at[step], recv_second.at[vector, peer], peer).wait_recv()
            pltpu.make_async_copy(
                send.at[:, mine, vector], second_ref.at[me, :, :, vector], own_second.at[vector]
            ).wait()

        def screen_vector(vector, carry):
            arrive(vector)

            def load(peer, inner):
                pltpu.make_async_copy(
                    second_ref.at[peer, :, :, vector], held.at[pl.ds(peer * CHUNKS, CHUNKS)], load_sem
                ).start()
                return inner

            lax.fori_loop(0, PEERS, load, 0)
            pltpu.make_async_copy(first_ref.at[0], held, load_sem).wait()

            def screen_one(freq, inner):
                assemble(
                    lambda peer, part, side: held[
                        pl.ds(peer * CHUNKS, CHUNKS), freq, part, side
                    ].reshape(HALF, TILE),
                    corr,
                )
                screen_one_matrix(coulomb_ref, corr, mixed, early_ref.at[freq, vector])
                return inner

            lax.fori_loop(0, freqs, screen_one, 0)
            return carry

        lax.fori_loop(0, vectors - 1, screen_vector, 0)
        arrive(vectors - 1)
        for step in range(PEERS - 1):
            peer = peer_at(me, step)
            remote_copy(
                send.at[:, pl.ds(peer * freqs, freqs)], second_ref.at[me], send_second.at[step],
                recv_second.at[0, me], peer,
            ).wait_send()


def exchange(partner, dyson, guess, coulomb, freq_index):
    freqs, vectors, _, size, _ = dyson.shape
    whole = freqs * PEERS
    block = pl.BlockSpec((1, 1, 2, size, size), lambda g: (g // vectors, g % vectors, 0, 0, 0))
    share = (2, 2, CHUNK, TILE)
    return pl.pallas_call(
        functools.partial(exchange_kernel, freqs, vectors),
        out_shape=[
            jax.ShapeDtypeStruct((CHUNKS, whole, vectors) + share, jnp.bfloat16),
            jax.ShapeDtypeStruct((PEERS, CHUNKS, freqs, vectors) + share, jnp.bfloat16),
            pltpu.VMEM((freqs, vectors - 1, 2, size, size), jnp.bfloat16),
        ],
        grid=(freqs * vectors,),
        in_specs=[
            pl.BlockSpec(memory_space=pltpu.SMEM),
            pl.BlockSpec(freq_index.shape, lambda g: (0, 0)),
            pl.BlockSpec(coulomb.shape, lambda g: (0, 0)),
            block,
            block,
        ],
        out_specs=[pl.BlockSpec(memory_space=pl.ANY)] * 2 + [pl.BlockSpec(memory_space=pltpu.VMEM)],
        scratch_shapes=[
            pltpu.VMEM((2, size, size), jnp.bfloat16),
            pltpu.VMEM((2, size, size), jnp.float32),
            pltpu.VMEM((CHUNKS, whole, vectors) + share, jnp.bfloat16),
            pltpu.VMEM((whole, vectors) + share, jnp.bfloat16),
            pltpu.VMEM((vectors, whole * 2 * 2 * CHUNK, TILE), jnp.float32),
            pltpu.VMEM((vectors, 4 * NT, 2 * GROUP * TILE), jnp.float32),
            pltpu.VMEM((4 * NT, 2 * whole), jnp.bfloat16),
            pltpu.VMEM((2 * whole, 2 * NT), jnp.bfloat16),
            pltpu.VMEM((size, size), jnp.bfloat16),
            pltpu.SemaphoreType.DMA((CHUNKS, PEERS - 1)),
            pltpu.SemaphoreType.DMA((CHUNKS, PEERS)),
            pltpu.SemaphoreType.DMA((CHUNKS,)),
            pltpu.SemaphoreType.DMA((PEERS - 1,)),
            pltpu.SemaphoreType.DMA((vectors, PEERS)),
            pltpu.SemaphoreType.DMA((vectors,)),
            pltpu.SemaphoreType.DMA,
        ],
        compiler_params=pltpu.CompilerParams(
            collective_id=0, has_side_effects=True, vmem_limit_bytes=EXCHANGE_LIMIT
        ),
    )(partner, freq_index, coulomb, dyson, guess)


def assemble(rows_of, polar):
    line, column = fold_indices()
    for part in range(2):
        for index, (low, high) in enumerate(PAIRS):
            for half in range(2):
                polar[part, pl.ds(low * TILE + half * HALF, HALF), pl.ds(high * TILE, TILE)] = rows_of(
                    2 * index + half, part, 0
                )
            lower = jnp.concatenate([rows_of(2 * index + half, part, 1) for half in range(2)], axis=0)
            polar[part, pl.ds(high * TILE, TILE), pl.ds(low * TILE, TILE)] = (
                lower.astype(jnp.float32).T.astype(jnp.bfloat16)
            )
        for block in range(4):
            plain = rows_of(2 * len(PAIRS) + block, part, 0).astype(jnp.float32)
            mirrored = rows_of(2 * len(PAIRS) + block, part, 1).astype(jnp.float32)
            turned = jnp.concatenate([mirrored, mirrored], axis=0).T
            top = jnp.where(column >= line, plain, turned[:HALF])
            corner = column - HALF
            bottom = jnp.where(
                corner < 0,
                turned[HALF:],
                jnp.where(
                    corner < line,
                    pltpu.roll(plain, HALF, 1),
                    jnp.where(corner == line, pltpu.roll(mirrored, HALF, 1), turned[:HALF]),
                ),
            )
            span = pl.ds(block * TILE, TILE)
            polar[part, span, span] = jnp.concatenate([top, bottom], axis=0).astype(jnp.bfloat16)


def screen_one_matrix(coulomb_ref, polar, mixed, out_ref):
    size = coulomb_ref.shape[0]
    for part in range(2):
        for row in range(0, size, 256):
            rows = pl.ds(row, 256)
            mixed[rows, :] = dot(coulomb_ref[rows, :], polar[part]).astype(jnp.bfloat16)
        for row in range(0, size, 256):
            rows = pl.ds(row, 256)
            product = dot(mixed[rows, :], coulomb_ref[...])
            if part == 0:
                product = product + coulomb_ref[rows, :].astype(jnp.float32)
            out_ref[part, rows, :] = product.astype(jnp.bfloat16)


def finish_kernel(blocks_ref, coulomb_ref, early_ref, out_ref, polar, mixed, result, early_sem, result_sem):
    freq = pl.program_id(0)
    freqs, early = early_ref.shape[0], early_ref.shape[1]

    def store_early(index):
        return pltpu.make_async_copy(
            early_ref.at[index], out_ref.at[index, pl.ds(0, early)], early_sem.at[index]
        )

    def store(index):
        return pltpu.make_async_copy(result.at[index], out_ref.at[index, early], result_sem.at[index])

    @pl.when(freq == 0)
    def _():
        for index in range(freqs):
            store_early(index).start()

    assemble(lambda peer, part, side: blocks_ref[peer, :, 0, 0, part, side].reshape(HALF, TILE), polar)
    screen_one_matrix(coulomb_ref, polar, mixed, result.at[freq])
    store(freq).start()

    @pl.when(freq == freqs - 1)
    def _():
        for index in range(freqs):
            store(index).wait()
            store_early(index).wait()


def finish(blocks, early, coulomb):
    _, _, freqs, vectors, _, _, _, _ = blocks.shape
    size = coulomb.shape[0]
    return pl.pallas_call(
        finish_kernel,
        out_shape=jax.ShapeDtypeStruct((freqs, vectors, 2, size, size), jnp.bfloat16),
        grid=(freqs,),
        in_specs=[
            pl.BlockSpec(
                (PEERS, CHUNKS, 1, 1, 2, 2, CHUNK, TILE), lambda v: (0, 0, v, vectors - 1, 0, 0, 0, 0)
            ),
            pl.BlockSpec((size, size), lambda v: (0, 0)),
            pl.BlockSpec(memory_space=pltpu.VMEM),
        ],
        out_specs=pl.BlockSpec(memory_space=pl.ANY),
        scratch_shapes=[
            pltpu.VMEM((2, size, size), jnp.bfloat16),
            pltpu.VMEM((size, size), jnp.bfloat16),
            pltpu.VMEM((freqs, 2, size, size), jnp.bfloat16),
            pltpu.SemaphoreType.DMA((freqs,)),
            pltpu.SemaphoreType.DMA((freqs,)),
        ],
        compiler_params=pltpu.CompilerParams(vmem_limit_bytes=VMEM_LIMIT),
    )(blocks, coulomb, early)


def local_paired(dyson, guess, coulomb, partner, freq_index):
    _, polar, early = exchange(partner, dyson, guess, coulomb, freq_index)
    return finish(polar, early, coulomb)


def solution(mesh):
    in_specs = (
        P(("groups", "freq"), None, None, None, None),
        P(("groups", "freq"), None, None, None, None),
        P("groups", None),
        P(),
        P(),
    )
    out_specs = P(("groups", "freq"), None, None, None, None)
    body = local_paired if mesh.shape["freq"] == PEERS else local
    return jax.shard_map(body, mesh=mesh, in_specs=in_specs, out_specs=out_specs, check_vma=False)
```

```python
import functools
import math

import jax
import jax.numpy as jnp
from jax import lax
from jax.experimental import pallas as pl
from jax.experimental.pallas import tpu as pltpu
from jax.sharding import PartitionSpec as P

NT = 64


def fermion_table(freq_index, time_count):
    freq_count = freq_index.shape[1]
    odd_freq = 2 * freq_index[0] + 1
    odd_time = 2 * jnp.arange(time_count, dtype=jnp.int32) + 1
    phases = jnp.mod(odd_time[:, None] * odd_freq[None, :], 4 * time_count)
    angles = phases.astype(jnp.float32) * (math.pi / (2 * time_count))
    cosine = jnp.cos(angles) / math.sqrt(freq_count)
    sine_part = jnp.sin(angles) / math.sqrt(freq_count)
    real_rows = jnp.stack([cosine, sine_part], axis=-1)
    imag_rows = jnp.stack([-sine_part, cosine], axis=-1)
    return jnp.stack([real_rows, imag_rows], axis=1).astype(jnp.bfloat16)


def boson_table(freq_index, time_count):
    odd_time = 2 * jnp.arange(time_count, dtype=jnp.int32) + 1
    phases = jnp.mod(freq_index[1][:, None] * odd_time[None, :], 2 * time_count)
    angles = phases.astype(jnp.float32) * (math.pi / time_count)
    cosine = jnp.cos(angles) / math.sqrt(time_count)
    sine_part = jnp.sin(angles) / math.sqrt(time_count)
    real_rows = jnp.stack([cosine, -sine_part], axis=-1)
    imag_rows = jnp.stack([sine_part, cosine], axis=-1)
    return jnp.stack([real_rows, imag_rows], axis=1).astype(jnp.bfloat16)


def batched(left_matrix, right_matrix):
    return jnp.einsum("bij,bjk->bik", left_matrix, right_matrix, preferred_element_type=jnp.float32)


def newton_green(dyson, guess):
    full_shape = dyson.shape
    batch_size = full_shape[0] * full_shape[1]
    matrix_size = full_shape[3]
    flat_dyson = dyson.reshape(batch_size, 2, matrix_size, matrix_size)
    flat_guess = guess.reshape(batch_size, 2, matrix_size, matrix_size)
    dyson_real, dyson_imag = (flat_dyson[:, 0], flat_dyson[:, 1])
    guess_real, guess_imag = (flat_guess[:, 0], flat_guess[:, 1])
    product_real = batched(dyson_real, guess_real) - batched(dyson_imag, guess_imag)
    product_imag = batched(dyson_real, guess_imag) + batched(dyson_imag, guess_real)
    unit_matrix = jnp.eye(matrix_size, dtype=jnp.float32)
    corr_real = (2.0 * unit_matrix - product_real).astype(jnp.bfloat16)
    corr_imag = (-product_imag).astype(jnp.bfloat16)
    green_real = batched(guess_real, corr_real) - batched(guess_imag, corr_imag)
    green_imag = batched(guess_real, corr_imag) + batched(guess_imag, corr_real)
    green_freq = jnp.stack([green_real, green_imag], axis=1).astype(jnp.bfloat16)
    return green_freq.reshape(full_shape)


def to_time(phase_table, values):
    return jnp.einsum("tdwc,wrcse->trdse", phase_table, values, preferred_element_type=jnp.float32)


def to_freq(phase_table, values):
    return jnp.einsum("vdtc,trcse->vrdse", phase_table, values, preferred_element_type=jnp.float32)


def polarize(green_time, hole_time):
    green_real, green_imag = (green_time[:, :, 0], green_time[:, :, 1])
    hole_real, hole_imag = (hole_time[:, :, 0], hole_time[:, :, 1])
    polar_real = green_real * hole_real - green_imag * hole_imag
    polar_imag = green_real * hole_imag + green_imag * hole_real
    return jnp.stack([polar_real, polar_imag], axis=2).astype(jnp.bfloat16)


def screen_block(polar_freq, coulomb):
    screened_polar = jnp.einsum(
        "ij,frcjk->frcik", coulomb, polar_freq, preferred_element_type=jnp.float32
    )
    screened_polar = screened_polar.astype(jnp.bfloat16)
    product = jnp.einsum(
        "frcij,jk->frcik", screened_polar, coulomb, preferred_element_type=jnp.float32
    )
    real_mask = (jnp.arange(2) == 0).astype(jnp.float32)[None, None, :, None, None]
    return (product + real_mask * coulomb.astype(jnp.float32)[None, None, None]).astype(
        jnp.bfloat16
    )


def take_vectors(values, partner):
    return jnp.concatenate(
        [lax.dynamic_slice_in_dim(values, partner[r], 1, axis=1) for r in range(values.shape[1])], axis=1
    )


def local(dyson, guess, coulomb, partner, freq_index):
    green_freq = newton_green(dyson, guess)
    forward = fermion_table(freq_index, NT)
    backward = boson_table(freq_index, NT)
    hole_freq = jnp.swapaxes(take_vectors(green_freq, partner), 3, 4)
    green_part = lax.all_to_all(green_freq, "freq", split_axis=3, concat_axis=0, tiled=True)
    hole_part = lax.all_to_all(hole_freq, "freq", split_axis=3, concat_axis=0, tiled=True)
    green_time = to_time(forward, green_part)
    hole_time = to_time(forward, hole_part)[::-1]
    polar_freq = to_freq(backward, polarize(green_time, hole_time)).astype(jnp.bfloat16)
    return screen_block(
        lax.all_to_all(polar_freq, "freq", split_axis=0, concat_axis=3, tiled=True), coulomb
    )


MESH = pl.DeviceIdType.MESH
PEERS = 16
TILE = 128
HALF = 64
PAIRS = [(0, 1), (0, 2), (0, 3), (1, 2), (1, 3), (2, 3)]
VMEM_LIMIT = 24 * 2**20
EXCHANGE_LIMIT = 42 * 2**20
CHUNK = 16
CHUNKS = HALF // CHUNK
GROUP = 4


def dot(left, right):
    return jnp.dot(left, right, preferred_element_type=jnp.float32)


def greet_all(me):
    barrier = pltpu.get_barrier_semaphore()
    for step in range(1, PEERS):
        peer = lax.rem(me + step, PEERS)
        pl.semaphore_signal(barrier, inc=1, device_id={"freq": peer}, device_id_type=MESH)


def await_greetings():
    pl.semaphore_wait(pltpu.get_barrier_semaphore(), PEERS - 1)


def peer_at(me, step):
    layer, place = me // 4, lax.rem(me, 4)
    side = layer // 2
    if step < 8:
        turn = step // 2
        if step % 2 == 0:
            return 12 * (1 - side) + lax.rem(place + turn, 4)
        return 8 - 4 * side + lax.rem(place + turn, 4)
    turn = step % 4
    if step < 12:
        return 4 * (layer + 1 - 2 * lax.rem(layer, 2)) + lax.rem(place + turn, 4)
    return 4 * layer + lax.rem(place + turn + 1, 4)


def remote_copy(source, target, send_sem, recv_sem, peer):
    return pltpu.make_async_remote_copy(
        src_ref=source,
        dst_ref=target,
        send_sem=send_sem,
        recv_sem=recv_sem,
        device_id={"freq": peer},
        device_id_type=MESH,
    )


def newton_step(dyson_ref, guess_ref, corr, green):
    size = dyson_ref.shape[-1]
    guess_real, guess_imag = guess_ref[0, 0, 0], guess_ref[0, 0, 1]
    for row in range(0, size, 256):
        rows = pl.ds(row, 256)
        dyson_real, dyson_imag = dyson_ref[0, 0, 0, rows, :], dyson_ref[0, 0, 1, rows, :]
        line = lax.broadcasted_iota(jnp.int32, (256, size), 0) + row
        column = lax.broadcasted_iota(jnp.int32, (256, size), 1)
        twice = jnp.where(line == column, 2.0, 0.0).astype(jnp.float32)
        product_real = dot(dyson_real, guess_real) - dot(dyson_imag, guess_imag)
        product_imag = dot(dyson_real, guess_imag) + dot(dyson_imag, guess_real)
        corr[0, rows, :] = (twice - product_real).astype(jnp.bfloat16)
        corr[1, rows, :] = (-product_imag).astype(jnp.bfloat16)
    corr_real, corr_imag = corr[0], corr[1]
    for row in range(0, size, 256):
        rows = pl.ds(row, 256)
        left_real, left_imag = guess_ref[0, 0, 0, rows, :], guess_ref[0, 0, 1, rows, :]
        green[0, rows, :] = dot(left_real, corr_real) - dot(left_imag, corr_imag)
        green[1, rows, :] = dot(left_real, corr_imag) + dot(left_imag, corr_real)


def fold_indices():
    line = lax.broadcasted_iota(jnp.int32, (HALF, TILE), 0)
    column = lax.broadcasted_iota(jnp.int32, (HALF, TILE), 1)
    return line, column


def pack_step(green, send, freqs, freq, vector):
    line, column = fold_indices()

    def put(peer, part, side, values):
        values = values.astype(jnp.bfloat16)
        for chunk in range(CHUNKS):
            send[chunk, peer * freqs + freq, vector, part, side] = values[chunk * CHUNK:(chunk + 1) * CHUNK]

    for part in range(2):
        for index, (low, high) in enumerate(PAIRS):
            upper = green[part, pl.ds(low * TILE, TILE), pl.ds(high * TILE, TILE)]
            lower = green[part, pl.ds(high * TILE, TILE), pl.ds(low * TILE, TILE)].T
            for half in range(2):
                cut = slice(half * HALF, (half + 1) * HALF)
                put(2 * index + half, part, 0, upper[cut])
                put(2 * index + half, part, 1, lower[cut])
        for block in range(4):
            span = pl.ds(block * TILE, TILE)
            plain = green[part, span, span]
            turned = plain.T
            plain_low = pltpu.roll(plain[HALF:], HALF, 1)
            turned_low = pltpu.roll(turned[HALF:], HALF, 1)
            put(2 * len(PAIRS) + block, part, 0, jnp.where(column >= line, plain[:HALF], plain_low))
            put(
                2 * len(PAIRS) + block, part, 1,
                jnp.where(column > line, turned[:HALF], jnp.where(column == line, plain_low, turned_low)),
            )


def fill_tables(index_ref, forward_ref, backward_ref):
    freqs = index_ref.shape[1]
    count = 2 * freqs
    doubled = jnp.concatenate([index_ref[...], index_ref[...]], axis=1)

    def waves(odd_time, freq, steps):
        angles = jnp.bitwise_and(odd_time * freq, 2 * steps - 1).astype(jnp.float32) * (math.pi / steps)
        return jnp.cos(angles), jnp.sin(angles)

    line = lax.broadcasted_iota(jnp.int32, (4 * NT, count), 0)
    column = lax.broadcasted_iota(jnp.int32, (4 * NT, count), 1)
    time = lax.rem(line, NT)
    odd_time = 2 * jnp.where(line < 2 * NT, time, NT - 1 - time) + 1
    cosine, sine_part = waves(odd_time, 2 * doubled[0:1] + 1, 2 * NT)
    imag_row, imag_column = lax.rem(line, 2 * NT) >= NT, column >= freqs
    value = jnp.where(imag_row == imag_column, cosine, jnp.where(imag_row, -sine_part, sine_part))
    forward_ref[...] = (value / math.sqrt(freqs)).astype(jnp.bfloat16)

    line = lax.broadcasted_iota(jnp.int32, (2 * NT, count), 0)
    column = lax.broadcasted_iota(jnp.int32, (2 * NT, count), 1)
    cosine, sine_part = waves(2 * lax.rem(line, NT) + 1, doubled[1:2], NT)
    imag_row, imag_column = line >= NT, column >= freqs
    value = jnp.where(imag_row == imag_column, cosine, jnp.where(imag_row, -sine_part, sine_part))
    backward_ref[...] = (value / math.sqrt(NT)).T.astype(jnp.bfloat16)


def polar_chunk(chunk, me, partner_ref, forward_ref, backward_ref, held, wide, timed, send):
    freqs, vectors = held.shape[0], held.shape[1]
    times = backward_ref.shape[1] // 2
    lanes = GROUP * TILE
    stride = 4 * CHUNK

    def widen(vector, carry):
        wide[vector] = held[:, vector].reshape(freqs * stride, TILE).astype(jnp.float32)
        return carry

    lax.fori_loop(0, vectors, widen, 0)
    for start in range(0, CHUNK, GROUP):

        def transform(vector, carry):
            gathered = jnp.concatenate(
                [
                    jnp.concatenate(
                        [
                            wide[vector, pl.ds((2 * part + side) * CHUNK + start + k, freqs, stride=stride), :]
                            for side in range(2)
                            for k in range(GROUP)
                        ],
                        axis=1,
                    )
                    for part in range(2)
                ],
                axis=0,
            ).astype(jnp.bfloat16)
            timed[vector] = dot(forward_ref[...], gathered)
            return carry

        def product(vector, carry):
            other = partner_ref[vector]
            lane = lax.broadcasted_iota(jnp.int32, (times, lanes), 1)
            itself = (lax.rem(lane, TILE) == lax.div(lane, TILE) + chunk * CHUNK + start) & (me >= 2 * len(PAIRS))
            parts = []
            for side in range(2):
                here, there = pl.ds(side * lanes, lanes), pl.ds((1 - side) * lanes, lanes)
                green_real = timed[vector, pl.ds(0, times), here]
                green_imag = timed[vector, pl.ds(times, times), here]
                hole_real = jnp.where(
                    itself, timed[other, pl.ds(2 * times, times), here], timed[other, pl.ds(2 * times, times), there]
                )
                hole_imag = jnp.where(
                    itself, timed[other, pl.ds(3 * times, times), here], timed[other, pl.ds(3 * times, times), there]
                )
                parts.append(
                    jnp.concatenate(
                        [
                            green_real * hole_real - green_imag * hole_imag,
                            green_real * hole_imag + green_imag * hole_real,
                        ],
                        axis=0,
                    ).astype(jnp.bfloat16)
                )
            for side in range(2):
                result = dot(backward_ref[...], parts[side])
                for part in range(2):
                    for k in range(GROUP):
                        wide[vector, pl.ds((2 * part + side) * CHUNK + start + k, freqs, stride=stride), :] = result[
                            part * freqs:(part + 1) * freqs, k * TILE:(k + 1) * TILE
                        ]
            return carry

        lax.fori_loop(0, vectors, transform, 0)
        lax.fori_loop(0, vectors, product, 0)

    def narrow(vector, carry):
        send[chunk, :, vector] = wide[vector].astype(jnp.bfloat16).reshape(freqs, 2, 2, CHUNK, TILE)
        return carry

    lax.fori_loop(0, vectors, narrow, 0)


def exchange_kernel(
    freqs, vectors, partner_ref, index_ref, coulomb_ref, dyson_ref, guess_ref,
    first_ref, second_ref, early_ref, held,
    corr, green, send, wide, timed, forward_ref, backward_ref, mixed,
    send_first, recv_first, own_first, send_second, recv_second, own_second, load_sem,
):
    me = lax.axis_index("freq")
    grid_step = pl.program_id(0)
    steps = freqs * vectors
    freq, vector = grid_step // vectors, lax.rem(grid_step, vectors)
    mine = pl.ds(me * freqs, freqs)

    @pl.when(grid_step == 0)
    def _():
        greet_all(me)

    newton_step(dyson_ref, guess_ref, corr, green)
    pack_step(green, send, freqs, freq, vector)

    @pl.when(grid_step == 0)
    def _():
        await_greetings()

    for step in range(PEERS - 1):
        peer = peer_at(me, step)
        remote_copy(
            send.at[0, peer * freqs + freq, vector], first_ref.at[0, me * freqs + freq, vector],
            send_first.at[0, step], recv_first.at[0, me], peer,
        ).start()
    pltpu.make_async_copy(
        send.at[0, me * freqs + freq, vector], first_ref.at[0, me * freqs + freq, vector], own_first.at[0]
    ).start()

    @pl.when(grid_step == steps - 1)
    def _():
        def send_later(chunk, carry):
            for step in range(PEERS - 1):
                peer = peer_at(me, step)
                remote_copy(
                    send.at[chunk, pl.ds(peer * freqs, freqs)], first_ref.at[chunk, mine],
                    send_first.at[chunk, step], recv_first.at[chunk, me], peer,
                ).start()
            pltpu.make_async_copy(send.at[chunk, mine], first_ref.at[chunk, mine], own_first.at[chunk]).start()
            return carry

        lax.fori_loop(1, CHUNKS, send_later, 0)
        fill_tables(index_ref, forward_ref, backward_ref)

        def middle(chunk, carry):
            for step in range(PEERS - 1):
                peer = peer_at(me, step)
                theirs = pl.ds(peer * freqs, freqs)
                remote_copy(
                    send.at[chunk, theirs], first_ref.at[chunk, theirs],
                    send_first.at[chunk, step], recv_first.at[chunk, peer], peer,
                ).wait()
            pltpu.make_async_copy(send.at[chunk, mine], first_ref.at[chunk, mine], own_first.at[chunk]).wait()
            load = pltpu.make_async_copy(first_ref.at[chunk], held, load_sem)
            load.start()
            load.wait()
            polar_chunk(chunk, me, partner_ref, forward_ref, backward_ref, held, wide, timed, send)

            def send_back(vector, inner):
                for step in range(PEERS - 1):
                    peer = peer_at(me, step)
                    remote_copy(
                        send.at[chunk, pl.ds(peer * freqs, freqs), vector], second_ref.at[me, chunk, :, vector],
                        send_second.at[step], recv_second.at[vector, me], peer,
                    ).start()
                pltpu.make_async_copy(
                    send.at[chunk, mine, vector], second_ref.at[me, chunk, :, vector], own_second.at[vector]
                ).start()
                return inner

            lax.fori_loop(0, vectors, send_back, 0)
            return carry

        lax.fori_loop(0, CHUNKS, middle, 0)

        def arrive(vector):
            def load(peer):
                pltpu.make_async_copy(
                    second_ref.at[peer, :, :, vector], held.at[pl.ds(peer * CHUNKS, CHUNKS)], load_sem
                ).start()

            pltpu.make_async_copy(
                send.at[:, mine, vector], second_ref.at[me, :, :, vector], own_second.at[vector]
            ).wait()
            load(me)
            for step in reversed(range(PEERS - 1)):
                peer = peer_at(me, step)
                slab = second_ref.at[peer, :, :, vector]
                remote_copy(slab, slab, send_second.at[step], recv_second.at[vector, peer], peer).wait_recv()
                load(peer)
            pltpu.make_async_copy(first_ref.at[0], held, load_sem).wait()

        def screen_vector(vector, carry):
            arrive(vector)

            def screen_one(freq, inner):
                assemble(
                    lambda peer, part, side: held[
                        pl.ds(peer * CHUNKS, CHUNKS), freq, part, side
                    ].reshape(HALF, TILE),
                    corr,
                )
                screen_one_matrix(coulomb_ref, corr, mixed, early_ref.at[freq, vector])
                return inner

            lax.fori_loop(0, freqs, screen_one, 0)
            return carry

        lax.fori_loop(0, vectors - 1, screen_vector, 0)
        arrive(vectors - 1)
        for step in range(PEERS - 1):
            peer = peer_at(me, step)
            remote_copy(
                send.at[:, pl.ds(peer * freqs, freqs)], second_ref.at[me], send_second.at[step],
                recv_second.at[0, me], peer,
            ).wait_send()


def exchange(partner, dyson, guess, coulomb, freq_index):
    freqs, vectors, _, size, _ = dyson.shape
    whole = freqs * PEERS
    block = pl.BlockSpec((1, 1, 2, size, size), lambda g: (g // vectors, g % vectors, 0, 0, 0))
    share = (2, 2, CHUNK, TILE)
    return pl.pallas_call(
        functools.partial(exchange_kernel, freqs, vectors),
        out_shape=[
            jax.ShapeDtypeStruct((CHUNKS, whole, vectors) + share, jnp.bfloat16),
            jax.ShapeDtypeStruct((PEERS, CHUNKS, freqs, vectors) + share, jnp.bfloat16),
            pltpu.VMEM((freqs, vectors - 1, 2, size, size), jnp.bfloat16),
            pltpu.VMEM((whole, vectors) + share, jnp.bfloat16),
        ],
        grid=(freqs * vectors,),
        in_specs=[
            pl.BlockSpec(memory_space=pltpu.SMEM),
            pl.BlockSpec(freq_index.shape, lambda g: (0, 0)),
            pl.BlockSpec(coulomb.shape, lambda g: (0, 0)),
            block,
            block,
        ],
        out_specs=[pl.BlockSpec(memory_space=pl.ANY)] * 2 + [pl.BlockSpec(memory_space=pltpu.VMEM)] * 2,
        scratch_shapes=[
            pltpu.VMEM((2, size, size), jnp.bfloat16),
            pltpu.VMEM((2, size, size), jnp.float32),
            pltpu.VMEM((CHUNKS, whole, vectors) + share, jnp.bfloat16),
            pltpu.VMEM((vectors, whole * 2 * 2 * CHUNK, TILE), jnp.float32),
            pltpu.VMEM((vectors, 4 * NT, 2 * GROUP * TILE), jnp.float32),
            pltpu.VMEM((4 * NT, 2 * whole), jnp.bfloat16),
            pltpu.VMEM((2 * whole, 2 * NT), jnp.bfloat16),
            pltpu.VMEM((size, size), jnp.bfloat16),
            pltpu.SemaphoreType.DMA((CHUNKS, PEERS - 1)),
            pltpu.SemaphoreType.DMA((CHUNKS, PEERS)),
            pltpu.SemaphoreType.DMA((CHUNKS,)),
            pltpu.SemaphoreType.DMA((PEERS - 1,)),
            pltpu.SemaphoreType.DMA((vectors, PEERS)),
            pltpu.SemaphoreType.DMA((vectors,)),
            pltpu.SemaphoreType.DMA,
        ],
        compiler_params=pltpu.CompilerParams(
            collective_id=0, has_side_effects=True, vmem_limit_bytes=EXCHANGE_LIMIT
        ),
    )(partner, freq_index, coulomb, dyson, guess)


def assemble(rows_of, polar):
    line, column = fold_indices()
    for part in range(2):
        for index, (low, high) in enumerate(PAIRS):
            for half in range(2):
                polar[part, pl.ds(low * TILE + half * HALF, HALF), pl.ds(high * TILE, TILE)] = rows_of(
                    2 * index + half, part, 0
                )
            lower = jnp.concatenate([rows_of(2 * index + half, part, 1) for half in range(2)], axis=0)
            polar[part, pl.ds(high * TILE, TILE), pl.ds(low * TILE, TILE)] = (
                lower.astype(jnp.float32).T.astype(jnp.bfloat16)
            )
        for block in range(4):
            plain = rows_of(2 * len(PAIRS) + block, part, 0).astype(jnp.float32)
            mirrored = rows_of(2 * len(PAIRS) + block, part, 1).astype(jnp.float32)
            turned = jnp.concatenate([mirrored, mirrored], axis=0).T
            top = jnp.where(column >= line, plain, turned[:HALF])
            corner = column - HALF
            bottom = jnp.where(
                corner < 0,
                turned[HALF:],
                jnp.where(
                    corner < line,
                    pltpu.roll(plain, HALF, 1),
                    jnp.where(corner == line, pltpu.roll(mirrored, HALF, 1), turned[:HALF]),
                ),
            )
            span = pl.ds(block * TILE, TILE)
            polar[part, span, span] = jnp.concatenate([top, bottom], axis=0).astype(jnp.bfloat16)


def screen_one_matrix(coulomb_ref, polar, mixed, out_ref):
    size = coulomb_ref.shape[0]
    for part in range(2):
        for row in range(0, size, 256):
            rows = pl.ds(row, 256)
            mixed[rows, :] = dot(coulomb_ref[rows, :], polar[part]).astype(jnp.bfloat16)
        for row in range(0, size, 256):
            rows = pl.ds(row, 256)
            product = dot(mixed[rows, :], coulomb_ref[...])
            if part == 0:
                product = product + coulomb_ref[rows, :].astype(jnp.float32)
            out_ref[part, rows, :] = product.astype(jnp.bfloat16)


def finish_kernel(held, coulomb_ref, early_ref, out_ref, polar, mixed, result, early_sem, result_sem):
    freqs, early = early_ref.shape[0], early_ref.shape[1]

    def store_early(index):
        return pltpu.make_async_copy(
            early_ref.at[index], out_ref.at[index, pl.ds(0, early)], early_sem.at[index]
        )

    def store(index):
        return pltpu.make_async_copy(result.at[index], out_ref.at[index, early], result_sem.at[index])

    for index in range(freqs):
        store_early(index).start()

    def screen_one(freq, carry):
        assemble(
            lambda peer, part, side: held[pl.ds(peer * CHUNKS, CHUNKS), freq, part, side].reshape(HALF, TILE),
            polar,
        )
        screen_one_matrix(coulomb_ref, polar, mixed, result.at[freq])
        store(freq).start()
        return carry

    lax.fori_loop(0, freqs, screen_one, 0)
    for index in range(freqs):
        store(index).wait()
        store_early(index).wait()


def finish(held, early, coulomb):
    freqs, known = early.shape[0], early.shape[1]
    size = coulomb.shape[0]
    return pl.pallas_call(
        finish_kernel,
        out_shape=jax.ShapeDtypeStruct((freqs, known + 1, 2, size, size), jnp.bfloat16),
        in_specs=[pl.BlockSpec(memory_space=pltpu.VMEM)] * 3,
        out_specs=pl.BlockSpec(memory_space=pl.ANY),
        scratch_shapes=[
            pltpu.VMEM((2, size, size), jnp.bfloat16),
            pltpu.VMEM((size, size), jnp.bfloat16),
            pltpu.VMEM((freqs, 2, size, size), jnp.bfloat16),
            pltpu.SemaphoreType.DMA((freqs,)),
            pltpu.SemaphoreType.DMA((freqs,)),
        ],
        compiler_params=pltpu.CompilerParams(vmem_limit_bytes=VMEM_LIMIT),
    )(held, coulomb, early)


def local_paired(dyson, guess, coulomb, partner, freq_index):
    _, _, early, held = exchange(partner, dyson, guess, coulomb, freq_index)
    return finish(held, early, coulomb)


def solution(mesh):
    in_specs = (
        P(("groups", "freq"), None, None, None, None),
        P(("groups", "freq"), None, None, None, None),
        P("groups", None),
        P(),
        P(),
    )
    out_specs = P(("groups", "freq"), None, None, None, None)
    body = local_paired if mesh.shape["freq"] == PEERS else local
    return jax.shard_map(body, mesh=mesh, in_specs=in_specs, out_specs=out_specs, check_vma=False)
```

```python
import functools
import math

import jax
import jax.numpy as jnp
from jax import lax
from jax.experimental import pallas as pl
from jax.experimental.pallas import tpu as pltpu
from jax.sharding import PartitionSpec as P

NT = 64


def fermion_table(freq_index, time_count):
    freq_count = freq_index.shape[1]
    odd_freq = 2 * freq_index[0] + 1
    odd_time = 2 * jnp.arange(time_count, dtype=jnp.int32) + 1
    phases = jnp.mod(odd_time[:, None] * odd_freq[None, :], 4 * time_count)
    angles = phases.astype(jnp.float32) * (math.pi / (2 * time_count))
    cosine = jnp.cos(angles) / math.sqrt(freq_count)
    sine_part = jnp.sin(angles) / math.sqrt(freq_count)
    real_rows = jnp.stack([cosine, sine_part], axis=-1)
    imag_rows = jnp.stack([-sine_part, cosine], axis=-1)
    return jnp.stack([real_rows, imag_rows], axis=1).astype(jnp.bfloat16)


def boson_table(freq_index, time_count):
    odd_time = 2 * jnp.arange(time_count, dtype=jnp.int32) + 1
    phases = jnp.mod(freq_index[1][:, None] * odd_time[None, :], 2 * time_count)
    angles = phases.astype(jnp.float32) * (math.pi / time_count)
    cosine = jnp.cos(angles) / math.sqrt(time_count)
    sine_part = jnp.sin(angles) / math.sqrt(time_count)
    real_rows = jnp.stack([cosine, -sine_part], axis=-1)
    imag_rows = jnp.stack([sine_part, cosine], axis=-1)
    return jnp.stack([real_rows, imag_rows], axis=1).astype(jnp.bfloat16)


def batched(left_matrix, right_matrix):
    return jnp.einsum("bij,bjk->bik", left_matrix, right_matrix, preferred_element_type=jnp.float32)


def newton_green(dyson, guess):
    full_shape = dyson.shape
    batch_size = full_shape[0] * full_shape[1]
    matrix_size = full_shape[3]
    flat_dyson = dyson.reshape(batch_size, 2, matrix_size, matrix_size)
    flat_guess = guess.reshape(batch_size, 2, matrix_size, matrix_size)
    dyson_real, dyson_imag = (flat_dyson[:, 0], flat_dyson[:, 1])
    guess_real, guess_imag = (flat_guess[:, 0], flat_guess[:, 1])
    product_real = batched(dyson_real, guess_real) - batched(dyson_imag, guess_imag)
    product_imag = batched(dyson_real, guess_imag) + batched(dyson_imag, guess_real)
    unit_matrix = jnp.eye(matrix_size, dtype=jnp.float32)
    corr_real = (2.0 * unit_matrix - product_real).astype(jnp.bfloat16)
    corr_imag = (-product_imag).astype(jnp.bfloat16)
    green_real = batched(guess_real, corr_real) - batched(guess_imag, corr_imag)
    green_imag = batched(guess_real, corr_imag) + batched(guess_imag, corr_real)
    green_freq = jnp.stack([green_real, green_imag], axis=1).astype(jnp.bfloat16)
    return green_freq.reshape(full_shape)


def to_time(phase_table, values):
    return jnp.einsum("tdwc,wrcse->trdse", phase_table, values, preferred_element_type=jnp.float32)


def to_freq(phase_table, values):
    return jnp.einsum("vdtc,trcse->vrdse", phase_table, values, preferred_element_type=jnp.float32)


def polarize(green_time, hole_time):
    green_real, green_imag = (green_time[:, :, 0], green_time[:, :, 1])
    hole_real, hole_imag = (hole_time[:, :, 0], hole_time[:, :, 1])
    polar_real = green_real * hole_real - green_imag * hole_imag
    polar_imag = green_real * hole_imag + green_imag * hole_real
    return jnp.stack([polar_real, polar_imag], axis=2).astype(jnp.bfloat16)


def screen_block(polar_freq, coulomb):
    screened_polar = jnp.einsum(
        "ij,frcjk->frcik", coulomb, polar_freq, preferred_element_type=jnp.float32
    )
    screened_polar = screened_polar.astype(jnp.bfloat16)
    product = jnp.einsum(
        "frcij,jk->frcik", screened_polar, coulomb, preferred_element_type=jnp.float32
    )
    real_mask = (jnp.arange(2) == 0).astype(jnp.float32)[None, None, :, None, None]
    return (product + real_mask * coulomb.astype(jnp.float32)[None, None, None]).astype(
        jnp.bfloat16
    )


def take_vectors(values, partner):
    return jnp.concatenate(
        [lax.dynamic_slice_in_dim(values, partner[r], 1, axis=1) for r in range(values.shape[1])], axis=1
    )


def local(dyson, guess, coulomb, partner, freq_index):
    green_freq = newton_green(dyson, guess)
    forward = fermion_table(freq_index, NT)
    backward = boson_table(freq_index, NT)
    hole_freq = jnp.swapaxes(take_vectors(green_freq, partner), 3, 4)
    green_part = lax.all_to_all(green_freq, "freq", split_axis=3, concat_axis=0, tiled=True)
    hole_part = lax.all_to_all(hole_freq, "freq", split_axis=3, concat_axis=0, tiled=True)
    green_time = to_time(forward, green_part)
    hole_time = to_time(forward, hole_part)[::-1]
    polar_freq = to_freq(backward, polarize(green_time, hole_time)).astype(jnp.bfloat16)
    return screen_block(
        lax.all_to_all(polar_freq, "freq", split_axis=0, concat_axis=3, tiled=True), coulomb
    )


MESH = pl.DeviceIdType.MESH
PEERS = 16
TILE = 128
HALF = 64
PAIRS = [(0, 1), (0, 2), (0, 3), (1, 2), (1, 3), (2, 3)]
VMEM_LIMIT = 24 * 2**20
EXCHANGE_LIMIT = 42 * 2**20
CHUNK = 16
CHUNKS = HALF // CHUNK
GROUP = 4


def dot(left, right):
    return jnp.dot(left, right, preferred_element_type=jnp.float32)


def greet_all(me):
    barrier = pltpu.get_barrier_semaphore()
    for step in range(1, PEERS):
        peer = lax.rem(me + step, PEERS)
        pl.semaphore_signal(barrier, inc=1, device_id={"freq": peer}, device_id_type=MESH)


def await_greetings():
    pl.semaphore_wait(pltpu.get_barrier_semaphore(), PEERS - 1)


def peer_at(me, step):
    layer, place = me // 4, lax.rem(me, 4)
    side = layer // 2
    if step < 8:
        turn = step // 2
        if step % 2 == 0:
            return 12 * (1 - side) + lax.rem(place + turn, 4)
        return 8 - 4 * side + lax.rem(place + turn, 4)
    turn = step % 4
    if step < 12:
        return 4 * (layer + 1 - 2 * lax.rem(layer, 2)) + lax.rem(place + turn, 4)
    return 4 * layer + lax.rem(place + turn + 1, 4)


def remote_copy(source, target, send_sem, recv_sem, peer):
    return pltpu.make_async_remote_copy(
        src_ref=source,
        dst_ref=target,
        send_sem=send_sem,
        recv_sem=recv_sem,
        device_id={"freq": peer},
        device_id_type=MESH,
    )


def newton_step(dyson_ref, guess_ref, corr, green):
    size = dyson_ref.shape[-1]
    guess_real, guess_imag = guess_ref[0, 0, 0], guess_ref[0, 0, 1]
    for row in range(0, size, 256):
        rows = pl.ds(row, 256)
        dyson_real, dyson_imag = dyson_ref[0, 0, 0, rows, :], dyson_ref[0, 0, 1, rows, :]
        line = lax.broadcasted_iota(jnp.int32, (256, size), 0) + row
        column = lax.broadcasted_iota(jnp.int32, (256, size), 1)
        twice = jnp.where(line == column, 2.0, 0.0).astype(jnp.float32)
        product_real = dot(dyson_real, guess_real) - dot(dyson_imag, guess_imag)
        product_imag = dot(dyson_real, guess_imag) + dot(dyson_imag, guess_real)
        corr[0, rows, :] = (twice - product_real).astype(jnp.bfloat16)
        corr[1, rows, :] = (-product_imag).astype(jnp.bfloat16)
    corr_real, corr_imag = corr[0], corr[1]
    for row in range(0, size, 256):
        rows = pl.ds(row, 256)
        left_real, left_imag = guess_ref[0, 0, 0, rows, :], guess_ref[0, 0, 1, rows, :]
        green[0, rows, :] = dot(left_real, corr_real) - dot(left_imag, corr_imag)
        green[1, rows, :] = dot(left_real, corr_imag) + dot(left_imag, corr_real)


def fold_indices():
    line = lax.broadcasted_iota(jnp.int32, (HALF, TILE), 0)
    column = lax.broadcasted_iota(jnp.int32, (HALF, TILE), 1)
    return line, column


def pack_step(green, send, freqs, freq, vector):
    line, column = fold_indices()

    def put(peer, part, side, values):
        values = values.astype(jnp.bfloat16)
        for chunk in range(CHUNKS):
            send[chunk, peer * freqs + freq, vector, part, side] = values[chunk * CHUNK:(chunk + 1) * CHUNK]

    for part in range(2):
        for index, (low, high) in enumerate(PAIRS):
            upper = green[part, pl.ds(low * TILE, TILE), pl.ds(high * TILE, TILE)]
            lower = green[part, pl.ds(high * TILE, TILE), pl.ds(low * TILE, TILE)].T
            for half in range(2):
                cut = slice(half * HALF, (half + 1) * HALF)
                put(2 * index + half, part, 0, upper[cut])
                put(2 * index + half, part, 1, lower[cut])
        for block in range(4):
            span = pl.ds(block * TILE, TILE)
            plain = green[part, span, span]
            turned = plain.T
            plain_low = pltpu.roll(plain[HALF:], HALF, 1)
            turned_low = pltpu.roll(turned[HALF:], HALF, 1)
            put(2 * len(PAIRS) + block, part, 0, jnp.where(column >= line, plain[:HALF], plain_low))
            put(
                2 * len(PAIRS) + block, part, 1,
                jnp.where(column > line, turned[:HALF], jnp.where(column == line, plain_low, turned_low)),
            )


def fill_tables(index_ref, forward_ref, backward_ref):
    freqs = index_ref.shape[1]
    count = 2 * freqs
    doubled = jnp.concatenate([index_ref[...], index_ref[...]], axis=1)

    def waves(odd_time, freq, steps):
        angles = jnp.bitwise_and(odd_time * freq, 2 * steps - 1).astype(jnp.float32) * (math.pi / steps)
        return jnp.cos(angles), jnp.sin(angles)

    line = lax.broadcasted_iota(jnp.int32, (4 * NT, count), 0)
    column = lax.broadcasted_iota(jnp.int32, (4 * NT, count), 1)
    time = lax.rem(line, NT)
    odd_time = 2 * jnp.where(line < 2 * NT, time, NT - 1 - time) + 1
    cosine, sine_part = waves(odd_time, 2 * doubled[0:1] + 1, 2 * NT)
    imag_row, imag_column = lax.rem(line, 2 * NT) >= NT, column >= freqs
    value = jnp.where(imag_row == imag_column, cosine, jnp.where(imag_row, -sine_part, sine_part))
    forward_ref[...] = (value / math.sqrt(freqs)).astype(jnp.bfloat16)

    line = lax.broadcasted_iota(jnp.int32, (2 * NT, count), 0)
    column = lax.broadcasted_iota(jnp.int32, (2 * NT, count), 1)
    cosine, sine_part = waves(2 * lax.rem(line, NT) + 1, doubled[1:2], NT)
    imag_row, imag_column = line >= NT, column >= freqs
    value = jnp.where(imag_row == imag_column, cosine, jnp.where(imag_row, -sine_part, sine_part))
    backward_ref[...] = (value / math.sqrt(NT)).T.astype(jnp.bfloat16)


def polar_chunk(chunk, me, partner_ref, forward_ref, backward_ref, held, wide, timed, send):
    freqs, vectors = held.shape[0], held.shape[1]
    times = backward_ref.shape[1] // 2
    lanes = GROUP * TILE
    stride = 4 * CHUNK

    def widen(vector, carry):
        wide[vector] = held[:, vector].reshape(freqs * stride, TILE).astype(jnp.float32)
        return carry

    lax.fori_loop(0, vectors, widen, 0)
    for start in range(0, CHUNK, GROUP):

        def transform(vector, carry):
            gathered = jnp.concatenate(
                [
                    jnp.concatenate(
                        [
                            wide[vector, pl.ds((2 * part + side) * CHUNK + start + k, freqs, stride=stride), :]
                            for side in range(2)
                            for k in range(GROUP)
                        ],
                        axis=1,
                    )
                    for part in range(2)
                ],
                axis=0,
            ).astype(jnp.bfloat16)
            timed[vector] = dot(forward_ref[...], gathered)
            return carry

        def product(vector, carry):
            other = partner_ref[vector]
            lane = lax.broadcasted_iota(jnp.int32, (times, lanes), 1)
            itself = (lax.rem(lane, TILE) == lax.div(lane, TILE) + chunk * CHUNK + start) & (me >= 2 * len(PAIRS))
            parts = []
            for side in range(2):
                here, there = pl.ds(side * lanes, lanes), pl.ds((1 - side) * lanes, lanes)
                green_real = timed[vector, pl.ds(0, times), here]
                green_imag = timed[vector, pl.ds(times, times), here]
                hole_real = jnp.where(
                    itself, timed[other, pl.ds(2 * times, times), here], timed[other, pl.ds(2 * times, times), there]
                )
                hole_imag = jnp.where(
                    itself, timed[other, pl.ds(3 * times, times), here], timed[other, pl.ds(3 * times, times), there]
                )
                parts.append(
                    jnp.concatenate(
                        [
                            green_real * hole_real - green_imag * hole_imag,
                            green_real * hole_imag + green_imag * hole_real,
                        ],
                        axis=0,
                    ).astype(jnp.bfloat16)
                )
            for side in range(2):
                result = dot(backward_ref[...], parts[side])
                for part in range(2):
                    for k in range(GROUP):
                        wide[vector, pl.ds((2 * part + side) * CHUNK + start + k, freqs, stride=stride), :] = result[
                            part * freqs:(part + 1) * freqs, k * TILE:(k + 1) * TILE
                        ]
            return carry

        lax.fori_loop(0, vectors, transform, 0)
        lax.fori_loop(0, vectors, product, 0)

    def narrow(vector, carry):
        send[chunk, :, vector] = wide[vector].astype(jnp.bfloat16).reshape(freqs, 2, 2, CHUNK, TILE)
        return carry

    lax.fori_loop(0, vectors, narrow, 0)


def exchange_kernel(
    freqs, vectors, partner_ref, index_ref, coulomb_ref, dyson_ref, guess_ref,
    first_ref, second_ref, early_ref, held,
    corr, green, send, wide, timed, forward_ref, backward_ref, mixed,
    send_first, recv_first, own_first, send_second, recv_second, own_second, load_sem,
):
    me = lax.axis_index("freq")
    grid_step = pl.program_id(0)
    steps = freqs * vectors
    freq, vector = grid_step // vectors, lax.rem(grid_step, vectors)
    mine = pl.ds(me * freqs, freqs)

    @pl.when(grid_step == 0)
    def _():
        greet_all(me)

    newton_step(dyson_ref, guess_ref, corr, green)
    pack_step(green, send, freqs, freq, vector)

    @pl.when(grid_step == 0)
    def _():
        await_greetings()

    for step in range(PEERS - 1):
        peer = peer_at(me, step)
        remote_copy(
            send.at[0, peer * freqs + freq, vector], first_ref.at[0, me * freqs + freq, vector],
            send_first.at[0, step], recv_first.at[0, me], peer,
        ).start()
    pltpu.make_async_copy(
        send.at[0, me * freqs + freq, vector], first_ref.at[0, me * freqs + freq, vector], own_first.at[0]
    ).start()

    @pl.when(grid_step == steps - 1)
    def _():
        def send_later(chunk, carry):
            for step in range(PEERS - 1):
                peer = peer_at(me, step)
                remote_copy(
                    send.at[chunk, pl.ds(peer * freqs, freqs)], first_ref.at[chunk, mine],
                    send_first.at[chunk, step], recv_first.at[chunk, me], peer,
                ).start()
            pltpu.make_async_copy(send.at[chunk, mine], first_ref.at[chunk, mine], own_first.at[chunk]).start()
            return carry

        lax.fori_loop(1, CHUNKS, send_later, 0)
        fill_tables(index_ref, forward_ref, backward_ref)

        def middle(chunk, carry):
            for step in range(PEERS - 1):
                peer = peer_at(me, step)
                theirs = pl.ds(peer * freqs, freqs)
                remote_copy(
                    send.at[chunk, theirs], first_ref.at[chunk, theirs],
                    send_first.at[chunk, step], recv_first.at[chunk, peer], peer,
                ).wait()
            pltpu.make_async_copy(send.at[chunk, mine], first_ref.at[chunk, mine], own_first.at[chunk]).wait()
            load = pltpu.make_async_copy(first_ref.at[chunk], held, load_sem)
            load.start()
            load.wait()
            polar_chunk(chunk, me, partner_ref, forward_ref, backward_ref, held, wide, timed, send)

            def send_back(vector, inner):
                for step in range(PEERS - 1):
                    peer = peer_at(me, step)
                    remote_copy(
                        send.at[chunk, pl.ds(peer * freqs, freqs), vector], second_ref.at[me, chunk, :, vector],
                        send_second.at[step], recv_second.at[vector, me], peer,
                    ).start()
                pltpu.make_async_copy(
                    send.at[chunk, mine, vector], second_ref.at[me, chunk, :, vector], own_second.at[vector]
                ).start()
                return inner

            lax.fori_loop(0, vectors, send_back, 0)
            return carry

        lax.fori_loop(0, CHUNKS, middle, 0)

        def arrive(vector):
            def load(peer):
                pltpu.make_async_copy(
                    second_ref.at[peer, :, :, vector], held.at[pl.ds(peer * CHUNKS, CHUNKS)], load_sem
                ).start()

            pltpu.make_async_copy(
                send.at[:, mine, vector], second_ref.at[me, :, :, vector], own_second.at[vector]
            ).wait()
            load(me)
            for step in reversed(range(PEERS - 1)):
                peer = peer_at(me, step)
                slab = second_ref.at[peer, :, :, vector]
                remote_copy(slab, slab, send_second.at[step], recv_second.at[vector, peer], peer).wait_recv()
                load(peer)
            pltpu.make_async_copy(first_ref.at[0], held, load_sem).wait()

        def screen_vector(vector, carry):
            arrive(vector)

            def screen_one(freq, inner):
                assemble(
                    lambda peer, part, side: held[
                        pl.ds(peer * CHUNKS, CHUNKS), freq, part, side
                    ].reshape(HALF, TILE),
                    corr,
                )
                screen_one_matrix(coulomb_ref, corr, mixed, early_ref.at[freq, vector])
                return inner

            lax.fori_loop(0, freqs, screen_one, 0)
            return carry

        lax.fori_loop(0, vectors - 1, screen_vector, 0)
        arrive(vectors - 1)
        for step in range(PEERS - 1):
            peer = peer_at(me, step)
            remote_copy(
                send.at[:, pl.ds(peer * freqs, freqs)], second_ref.at[me], send_second.at[step],
                recv_second.at[0, me], peer,
            ).wait_send()


def exchange(partner, dyson, guess, coulomb, freq_index):
    freqs, vectors, _, size, _ = dyson.shape
    whole = freqs * PEERS
    block = pl.BlockSpec((1, 1, 2, size, size), lambda g: (g // vectors, g % vectors, 0, 0, 0))
    share = (2, 2, CHUNK, TILE)
    return pl.pallas_call(
        functools.partial(exchange_kernel, freqs, vectors),
        out_shape=[
            jax.ShapeDtypeStruct((CHUNKS, whole, vectors) + share, jnp.bfloat16),
            jax.ShapeDtypeStruct((PEERS, CHUNKS, freqs, vectors) + share, jnp.bfloat16),
            pltpu.VMEM((freqs, vectors - 1, 2, size, size), jnp.bfloat16),
            pltpu.VMEM((whole, vectors) + share, jnp.bfloat16),
        ],
        grid=(freqs * vectors,),
        in_specs=[
            pl.BlockSpec(memory_space=pltpu.SMEM),
            pl.BlockSpec(freq_index.shape, lambda g: (0, 0)),
            pl.BlockSpec(coulomb.shape, lambda g: (0, 0)),
            block,
            block,
        ],
        out_specs=[pl.BlockSpec(memory_space=pl.ANY)] * 2 + [pl.BlockSpec(memory_space=pltpu.VMEM)] * 2,
        scratch_shapes=[
            pltpu.VMEM((2, size, size), jnp.bfloat16),
            pltpu.VMEM((2, size, size), jnp.float32),
            pltpu.VMEM((CHUNKS, whole, vectors) + share, jnp.bfloat16),
            pltpu.VMEM((vectors, whole * 2 * 2 * CHUNK, TILE), jnp.float32),
            pltpu.VMEM((vectors, 4 * NT, 2 * GROUP * TILE), jnp.float32),
            pltpu.VMEM((4 * NT, 2 * whole), jnp.bfloat16),
            pltpu.VMEM((2 * whole, 2 * NT), jnp.bfloat16),
            pltpu.VMEM((size, size), jnp.bfloat16),
            pltpu.SemaphoreType.DMA((CHUNKS, PEERS - 1)),
            pltpu.SemaphoreType.DMA((CHUNKS, PEERS)),
            pltpu.SemaphoreType.DMA((CHUNKS,)),
            pltpu.SemaphoreType.DMA((PEERS - 1,)),
            pltpu.SemaphoreType.DMA((vectors, PEERS)),
            pltpu.SemaphoreType.DMA((vectors,)),
            pltpu.SemaphoreType.DMA,
        ],
        compiler_params=pltpu.CompilerParams(
            collective_id=0, has_side_effects=True, vmem_limit_bytes=EXCHANGE_LIMIT
        ),
    )(partner, freq_index, coulomb, dyson, guess)


def assemble(rows_of, polar):
    line, column = fold_indices()
    for part in range(2):
        for index, (low, high) in enumerate(PAIRS):
            for half in range(2):
                polar[part, pl.ds(low * TILE + half * HALF, HALF), pl.ds(high * TILE, TILE)] = rows_of(
                    2 * index + half, part, 0
                )
            lower = jnp.concatenate([rows_of(2 * index + half, part, 1) for half in range(2)], axis=0)
            polar[part, pl.ds(high * TILE, TILE), pl.ds(low * TILE, TILE)] = (
                lower.astype(jnp.float32).T.astype(jnp.bfloat16)
            )
        for block in range(4):
            plain = rows_of(2 * len(PAIRS) + block, part, 0).astype(jnp.float32)
            mirrored = rows_of(2 * len(PAIRS) + block, part, 1).astype(jnp.float32)
            turned = jnp.concatenate([mirrored, mirrored], axis=0).T
            top = jnp.where(column >= line, plain, turned[:HALF])
            corner = column - HALF
            bottom = jnp.where(
                corner < 0,
                turned[HALF:],
                jnp.where(
                    corner < line,
                    pltpu.roll(plain, HALF, 1),
                    jnp.where(corner == line, pltpu.roll(mirrored, HALF, 1), turned[:HALF]),
                ),
            )
            span = pl.ds(block * TILE, TILE)
            polar[part, span, span] = jnp.concatenate([top, bottom], axis=0).astype(jnp.bfloat16)


def screen_one_matrix(coulomb_ref, polar, mixed, out_ref):
    size = coulomb_ref.shape[0]
    for part in range(2):
        for row in range(0, size, 256):
            rows = pl.ds(row, 256)
            mixed[rows, :] = dot(coulomb_ref[rows, :], polar[part]).astype(jnp.bfloat16)
        for row in range(0, size, 256):
            rows = pl.ds(row, 256)
            product = dot(mixed[rows, :], coulomb_ref[...])
            if part == 0:
                product = product + coulomb_ref[rows, :].astype(jnp.float32)
            out_ref[part, rows, :] = product.astype(jnp.bfloat16)


def finish_kernel(held, coulomb_ref, early_ref, out_ref, polar, mixed, result, early_sem, result_sem):
    freqs, early = early_ref.shape[0], early_ref.shape[1]

    def store_early(index):
        return pltpu.make_async_copy(
            early_ref.at[index], out_ref.at[index, pl.ds(0, early)], early_sem.at[index]
        )

    def store(index):
        return pltpu.make_async_copy(result.at[index], out_ref.at[index, early], result_sem.at[index])

    for index in range(freqs):
        store_early(index).start()

    def gather(freq):
        assemble(
            lambda peer, part, side: held[pl.ds(peer * CHUNKS, CHUNKS), freq, part, side].reshape(HALF, TILE),
            polar.at[freq % 2],
        )

    gather(0)
    for freq in range(freqs):
        if freq + 1 < freqs:
            gather(freq + 1)
        screen_one_matrix(coulomb_ref, polar.at[freq % 2], mixed.at[freq % 2], result.at[freq])
        store(freq).start()
    for index in range(freqs):
        store(index).wait()
        store_early(index).wait()


def finish(held, early, coulomb):
    freqs, known = early.shape[0], early.shape[1]
    size = coulomb.shape[0]
    return pl.pallas_call(
        finish_kernel,
        out_shape=jax.ShapeDtypeStruct((freqs, known + 1, 2, size, size), jnp.bfloat16),
        in_specs=[pl.BlockSpec(memory_space=pltpu.VMEM)] * 3,
        out_specs=pl.BlockSpec(memory_space=pl.ANY),
        scratch_shapes=[
            pltpu.VMEM((2, 2, size, size), jnp.bfloat16),
            pltpu.VMEM((2, size, size), jnp.bfloat16),
            pltpu.VMEM((freqs, 2, size, size), jnp.bfloat16),
            pltpu.SemaphoreType.DMA((freqs,)),
            pltpu.SemaphoreType.DMA((freqs,)),
        ],
        compiler_params=pltpu.CompilerParams(vmem_limit_bytes=VMEM_LIMIT),
    )(held, coulomb, early)


def local_paired(dyson, guess, coulomb, partner, freq_index):
    _, _, early, held = exchange(partner, dyson, guess, coulomb, freq_index)
    return finish(held, early, coulomb)


def solution(mesh):
    in_specs = (
        P(("groups", "freq"), None, None, None, None),
        P(("groups", "freq"), None, None, None, None),
        P("groups", None),
        P(),
        P(),
    )
    out_specs = P(("groups", "freq"), None, None, None, None)
    body = local_paired if mesh.shape["freq"] == PEERS else local
    return jax.shard_map(body, mesh=mesh, in_specs=in_specs, out_specs=out_specs, check_vma=False)
```
